32 devices in a mesh: seq: 8 (over z, x), head: 4 (over y, core).
Axes of the slice: x: 2, y: 2, z: 4, core: 2. Of those that a mesh axis runs over, the one named last changes fastest.
Arguments:
- queries: bfloat16 [1024, 2048], P('seq', 'head'), may hold values from -6 to 6
- keys: bfloat16 [1024, 2048], P('seq', 'head'), may hold values from -6 to 6
- values: bfloat16 [1024, 2048], P('seq', 'head'), may hold values from -7 to 7
- d_out: bfloat16 [1024, 2048], P('seq', 'head'), may hold values from -6 to 6
- gain: float32 [2048], P('head'), may hold values from 0.25 to 1.75
Outputs:
- normed: bfloat16 [1024, 2048], P('seq', 'head')
- query_grad: bfloat16 [1024, 2048], P('seq', 'head')
- key_grad: bfloat16 [1024, 2048], P('seq', 'head')
- value_grad: bfloat16 [1024, 2048], P('seq', 'head')
The draws below stay inside these ranges and needn't reach their ends.
All inputs are finite; a program needn't handle non-finite values.
Results may differ from the reference program's by a relative error of at most 0.0049.
Values sent between devices are 32-bit elements; how exact they have to be, the bound alone decides.
No kernel may reach another device: no remote copies, remote signals or barrier semaphores. Data moves between devices by JAX's collectives and lax.ppermute only.
A program may use at most 64 MiB of HBM per device.

```python
import math
import jax
import jax.numpy as jnp
from jax import lax

HEADS = 32
HEAD_DIM = 64
BLOCK = 128
TOKENS = 1024


def draw_values(key, part):
    position = jnp.arange(HEADS, dtype=jnp.float32) / (HEADS - 1)
    sample = jnp.clip(jax.random.normal(key, (TOKENS, HEADS, HEAD_DIM), jnp.float32), -4.0, 4.0)
    growth = 3.0 ** (0.5 * position)
    return (sample * growth[None, :, None]).reshape(TOKENS, HEADS * HEAD_DIM).astype(jnp.bfloat16)


def block_levels(stream_key, extent, shards, smallest, largest):
    factor_of = 1.0
    for dim, shards_of in shards:
        draws = jax.random.uniform(jax.random.fold_in(jax.random.fold_in(stream_key, 6), dim), (shards_of,), jnp.float32, smallest / len(shards), largest / len(shards))
        factor_of = factor_of * jnp.repeat(jnp.exp(draws), extent[dim] // shards_of).reshape((-1,) + (1,) * (len(extent) - 1 - dim))
    return factor_of


def bell_draw(own_key, dims, deviation, most, shards=(), kind=jnp.bfloat16):
    drawn = deviation * jax.random.normal(own_key, dims, jnp.float32)
    if shards:
        drawn = drawn * block_levels(own_key, dims, shards, -0.22, 0.18)
    return jnp.clip(drawn, -most, most).astype(kind)


def setup_inputs(seed: int = 0) -> dict:
    arg_keys = jax.random.split(jax.random.key(seed), 6)
    return {
        "queries": bell_draw(arg_keys[0], (TOKENS, HEADS * HEAD_DIM), 1.0, 6.0, ((0, 8), (1, 4))),
        "keys": bell_draw(arg_keys[1], (TOKENS, HEADS * HEAD_DIM), 1.0, 6.0, ((0, 8), (1, 4))),
        "values": draw_values(jax.random.fold_in(arg_keys[5], 71), 0),
        "d_out": bell_draw(arg_keys[3], (TOKENS, HEADS * HEAD_DIM), 1.0, 6.0, ((0, 8), (1, 4))),
        "gain": jnp.clip(1.0 + 0.15 * jax.random.normal(arg_keys[4], (HEADS * HEAD_DIM,), jnp.float32), 0.25, 1.75),
    }


def round_half(tensor):
    return lax.optimization_barrier(tensor.astype(jnp.bfloat16)).astype(jnp.float32)

def reference(queries, keys, values, d_out, gain):
    length = queries.shape[0]
    head_count = HEADS
    head_width = HEAD_DIM
    block_count = length // BLOCK
    factor = 1.0 / math.sqrt(head_width * length)
    row_index = lax.broadcasted_iota(jnp.int32, (BLOCK, BLOCK), 0)
    column_index = lax.broadcasted_iota(jnp.int32, (BLOCK, BLOCK), 1)
    causal = (row_index >= column_index)[None]
    gain_heads = gain.reshape(head_count, head_width)

    def blocks(tensor):
        return tensor.reshape(block_count, BLOCK, head_count, head_width)
    inputs = (blocks(queries), blocks(keys), blocks(values), blocks(d_out))

    def local_weights(query, key, value, grad):
        weights = round_half(factor * jnp.where(causal, jnp.einsum('ihd,jhd->hij', query, key), 0.0))
        dweights = round_half(factor * jnp.where(causal, jnp.einsum('ihe,jhe->hij', grad, value), 0.0))
        return (weights, dweights)

    def forward_step(carry, block):
        query, key, value, grad = [part.astype(jnp.float32) for part in block]
        weights, dweights = local_weights(query, key, value, grad)
        state = round_half(factor * carry)
        output = jnp.einsum('hij,jhe->ihe', weights, value) + jnp.einsum('ihd,hde->ihe', query, state)
        mean_square = lax.optimization_barrier(jnp.mean(output * output, axis=(1, 2)))
        normed = (output * lax.rsqrt(mean_square + 1e-06)[:, None, None] * gain_heads[None]).astype(jnp.bfloat16)
        query_grad = jnp.einsum('hij,jhd->ihd', dweights, key) + jnp.einsum('ihe,hde->ihd', grad, state)
        carry = carry + jnp.einsum('jhd,jhe->hde', key, value)
        return (carry, (normed, query_grad.astype(jnp.bfloat16)))

    def backward_step(carry, block):
        query, key, value, grad = [part.astype(jnp.float32) for part in block]
        weights, dweights = local_weights(query, key, value, grad)
        grad_state = round_half(factor * carry)
        key_grad = jnp.einsum('hij,ihd->jhd', dweights, query) + jnp.einsum('jhe,hed->jhd', value, grad_state)
        value_grad = jnp.einsum('hij,ihe->jhe', weights, grad) + jnp.einsum('jhd,hed->jhe', key, grad_state)
        carry = carry + jnp.einsum('ihe,ihd->hed', grad, query)
        return (carry, (key_grad.astype(jnp.bfloat16), value_grad.astype(jnp.bfloat16)))
    zeros = jnp.zeros((head_count, head_width, head_width), jnp.float32)
    unused, (normed, query_grad) = lax.scan(forward_step, zeros, inputs)
    unused, (key_grad, value_grad) = lax.scan(backward_step, zeros, inputs, reverse=True)
    shape = (length, head_count * head_width)
    return (normed.reshape(shape), query_grad.reshape(shape), key_grad.reshape(shape), value_grad.reshape(shape))
```

```python
import functools
import math

import jax
import jax.numpy as jnp
from jax import lax
from jax.experimental import pallas as pl
from jax.experimental.pallas import tpu as pltpu
from jax.sharding import PartitionSpec as P

HEAD_DIM = 64
BLOCK = 128
LANES = 128

epsilon = 1e-06


f32 = jnp.float32
bf16 = jnp.bfloat16


def dot(x, y, dims=((1,), (0,))):
    return lax.dot_general(x, y, (dims, ((), ())), preferred_element_type=f32)


NT = ((1,), (1,))
TN = ((0,), (0,))


def tiles(ref):
    return ref.shape[1] // LANES


def tile(ref, t):
    return ref[:, t * LANES : (t + 1) * LANES]


def lane_is_low(shape):
    return lax.broadcasted_iota(jnp.int32, shape, 1) < HEAD_DIM


def by_head(x):
    low = lane_is_low(x.shape)
    zero = jnp.zeros_like(x)
    return jnp.where(low, x, zero), jnp.where(low, zero, x)


def pack_state(product):
    low = lane_is_low((HEAD_DIM, LANES))
    return jnp.where(low, product[:HEAD_DIM], product[HEAD_DIM:])


def unpack_state(state):
    low = lane_is_low(state.shape)
    zero = jnp.zeros_like(state)
    return jnp.concatenate([jnp.where(low, state, zero), jnp.where(low, zero, state)], axis=0)


def states_kernel(q_ref, k_ref, v_ref, g_ref, kv_ref, qg_ref):
    for t in range(tiles(q_ref)):
        rows = slice(t * HEAD_DIM, (t + 1) * HEAD_DIM)
        kv_ref[rows] = pack_state(dot(tile(k_ref, t), tile(v_ref, t), TN))
        qg_ref[rows] = pack_state(dot(tile(g_ref, t), tile(q_ref, t), TN))


def block_kernel(factor, q_ref, k_ref, v_ref, g_ref, out_ref, dq_ref, dk_ref, dv_ref):
    row = lax.broadcasted_iota(jnp.int32, (BLOCK, BLOCK), 0)
    column = lax.broadcasted_iota(jnp.int32, (BLOCK, BLOCK), 1)
    causal = row >= column
    for t in range(tiles(q_ref)):
        q, k, v, g = (tile(ref, t) for ref in (q_ref, k_ref, v_ref, g_ref))
        cols = slice(t * LANES, (t + 1) * LANES)
        out = dq = dk = dv = None
        for qh, gh, kh, vh in zip(by_head(q), by_head(g), by_head(k), by_head(v)):
            weights = (factor * jnp.where(causal, dot(qh, k, NT), 0.0)).astype(bf16)
            dweights = (factor * jnp.where(causal, dot(gh, v, NT), 0.0)).astype(bf16)
            parts = (dot(weights, vh), dot(dweights, kh), dot(dweights, qh, TN), dot(weights, gh, TN))
            if out is None:
                out, dq, dk, dv = parts
            else:
                out, dq, dk, dv = (x + y for x, y in zip((out, dq, dk, dv), parts))
        out_ref[:, cols] = out
        dq_ref[:, cols] = dq
        dk_ref[:, cols] = dk
        dv_ref[:, cols] = dv


def output_kernel(factor, q_ref, part_ref, kv_ref, out_ref, squares_ref):
    total = None
    for t in range(tiles(q_ref)):
        cols = slice(t * LANES, (t + 1) * LANES)
        state = unpack_state((factor * kv_ref[t * HEAD_DIM : (t + 1) * HEAD_DIM]).astype(bf16))
        out = part_ref[:, cols] + dot(tile(q_ref, t), state)
        out_ref[:, cols] = out
        square = out * out
        total = square if total is None else total + square
    squares_ref[...] = jnp.sum(total.T, axis=0, keepdims=True)


def grads_kernel(
    factor, k_ref, v_ref, g_ref, dq_part, dk_part, dv_part, kv_ref, qg_ref, dq_ref, dk_ref, dv_ref
):
    for t in range(tiles(k_ref)):
        cols = slice(t * LANES, (t + 1) * LANES)
        rows = slice(t * HEAD_DIM, (t + 1) * HEAD_DIM)
        state = unpack_state((factor * kv_ref[rows]).astype(bf16))
        grad_state = unpack_state((factor * qg_ref[rows]).astype(bf16))
        dq_ref[:, cols] = (dq_part[:, cols] + dot(tile(g_ref, t), state, NT)).astype(bf16)
        dk_ref[:, cols] = (dk_part[:, cols] + dot(tile(v_ref, t), grad_state)).astype(bf16)
        dv_ref[:, cols] = (dv_part[:, cols] + dot(tile(k_ref, t), grad_state, NT)).astype(bf16)


def norm_kernel(width, out_ref, squares_ref, gain_ref, normed_ref):
    total = jnp.sum(squares_ref[...], axis=0, keepdims=True)
    scale = lax.rsqrt(total / width + epsilon)
    scale = jnp.broadcast_to(scale, (LANES, scale.shape[1])).T
    for t in range(tiles(out_ref)):
        cols = slice(t * LANES, (t + 1) * LANES)
        normed_ref[:, cols] = (out_ref[:, cols] * scale * gain_ref[:, cols]).astype(bf16)


def call(kernel, outs, args, flops):
    moved = sum(math.prod(a.shape) * jnp.dtype(a.dtype).itemsize for a in (*args, *outs))
    whole = pl.BlockSpec(memory_space=pltpu.VMEM)
    single = len(outs) == 1
    return pl.pallas_call(
        kernel,
        out_shape=outs[0] if single else tuple(outs),
        in_specs=[whole] * len(args),
        out_specs=whole if single else tuple([whole] * len(outs)),
        compiler_params=pltpu.CompilerParams(vmem_limit_bytes=16 * 2**20),
        cost_estimate=pl.CostEstimate(flops=flops, bytes_accessed=moved, transcendentals=0),
    )(*args)


def swap(x, axis, distance):
    size = lax.axis_size(axis)
    return lax.ppermute(x, axis, [(i, i ^ distance) for i in range(size)])


def halves(x, odd):
    mid = x.shape[0] // 2
    low, high = x[:mid], x[mid:]
    return jnp.where(odd, high, low), jnp.where(odd, low, high)


def join(mine, other, odd):
    return jnp.concatenate([jnp.where(odd, other, mine), jnp.where(odd, mine, other)], axis=0)


def scan_states(kv, qg, axis):
    count = lax.axis_size(axis)
    index = lax.axis_index(axis)
    bit = lambda d: (index & d) != 0
    zero = jnp.zeros_like(kv)
    top = count // 2
    if count & (count - 1):
        position = jnp.arange(count)[:, None, None]
        every_kv = lax.all_gather(kv, axis)
        every_qg = lax.all_gather(qg, axis)
        return (
            jnp.sum(jnp.where(position < index, every_kv, 0.0), axis=0),
            jnp.sum(jnp.where(position > index, every_qg, 0.0), axis=0),
        )
    if count < 8:
        before, after, total_kv, total_qg = zero, zero, kv, qg
        distance = 1
        while distance < count:
            got_kv, got_qg = swap(total_kv, axis, distance), swap(total_qg, axis, distance)
            before = before + jnp.where(bit(distance), got_kv, 0.0)
            after = after + jnp.where(bit(distance), 0.0, got_qg)
            total_kv, total_qg = total_kv + got_kv, total_qg + got_qg
            distance *= 2
        return before, after
    odd, upper = bit(1), bit(top)
    a, b = jnp.where(upper, qg, kv), jnp.where(upper, kv, qg)
    (a_mine, a_other), (b_mine, b_other) = halves(a, odd), halves(b, odd)
    a1 = swap(a_other, axis, 1)
    a2 = swap(a_mine, axis, 2)
    a3 = swap(a_other, axis, 3)
    b1 = swap(b_other, axis, 1)
    b2 = swap(b_mine, axis, 2)
    b3 = swap(b_other, axis, 3)
    a_enters = lambda d: bit(d) != upper
    b_enters = lambda d: bit(d) == upper
    a_pair, b_pair = a2 + a3, b2 + b3
    a_sum = jnp.where(a_enters(2), a_pair, 0.0)
    b_sum = jnp.where(b_enters(2), b_pair, 0.0)
    a_total, b_total = a_mine + a1 + a_pair, b_mine + b1 + b_pair
    distance = 4
    while distance < top:
        a_got, b_got = swap(a_total, axis, distance), swap(b_total, axis, distance)
        a_sum = a_sum + jnp.where(a_enters(distance), a_got, 0.0)
        b_sum = b_sum + jnp.where(b_enters(distance), b_got, 0.0)
        a_total, b_total = a_total + a_got, b_total + b_got
        distance *= 2
    t_mine = swap(a_total, axis, top)
    t_other = swap(a_total, axis, top | 1)
    a_out = a_sum + jnp.where(a_enters(1), 0.0, a_mine)
    b_out = b_sum + jnp.where(b_enters(1), 0.0, b_mine)
    got = swap(jnp.concatenate([a_out, b_out], axis=0), axis, 1)
    mid = a_mine.shape[0]
    a_own = a_sum + jnp.where(a_enters(1), a1, 0.0)
    b_own = b_sum + jnp.where(b_enters(1), b1, 0.0) + t_mine
    a_all = join(a_own, got[:mid], odd)
    b_all = join(b_own, got[mid:] + t_other, odd)
    return jnp.where(upper, b_all, a_all), jnp.where(upper, a_all, b_all)


def all_shares(row, axis):
    count = lax.axis_size(axis)
    if count & (count - 1):
        return lax.psum(row, axis)
    if count > 4:
        distance = 1
        while distance < count:
            row = row + swap(row, axis, distance)
            distance *= 2
        return row
    return jnp.concatenate([row] + [swap(row, axis, d) for d in range(1, count)], axis=0)


def body(queries, keys, values, d_out, gain):
    length, width = queries.shape
    factor = 1.0 / math.sqrt(HEAD_DIM * length * lax.axis_size("seq"))
    row_bytes = jax.ShapeDtypeStruct((width // LANES * HEAD_DIM, LANES), f32)
    wide = jax.ShapeDtypeStruct((length, width), f32)
    narrow = jax.ShapeDtypeStruct((length, width), bf16)
    inputs = (queries, keys, values, d_out)
    kv, qg = call(states_kernel, [row_bytes] * 2, inputs, 4 * length * LANES * width)
    out_part, dq_part, dk_part, dv_part = call(
        functools.partial(block_kernel, factor), [wide] * 4, inputs, 24 * length * LANES * width
    )
    before, after = scan_states(kv, qg, "seq")
    out, squares = call(
        functools.partial(output_kernel, factor),
        [wide, jax.ShapeDtypeStruct((1, length), f32)],
        (queries, out_part, before),
        2 * length * LANES * width,
    )
    shares = all_shares(squares, "head")
    dq, dk, dv = call(
        functools.partial(grads_kernel, factor),
        [narrow] * 3,
        (keys, values, d_out, dq_part, dk_part, dv_part, before, after),
        6 * length * LANES * width,
    )
    normed = call(
        functools.partial(norm_kernel, width * lax.axis_size("head")),
        [narrow],
        (out, shares, gain[None]),
        2 * length * width,
    )
    return normed, dq, dk, dv


def solution(mesh):
    placed = (P("seq", "head"), P("seq", "head"), P("seq", "head"), P("seq", "head"), P("head"))

    return jax.shard_map(
        body,
        mesh=mesh,
        in_specs=placed,
        out_specs=(P("seq", "head"), P("seq", "head"), P("seq", "head"), P("seq", "head")),
        check_vma=False,
    )
```

```python
import functools
import math

import jax
import jax.numpy as jnp
from jax import lax
from jax.experimental import pallas as pl
from jax.experimental.pallas import tpu as pltpu
from jax.sharding import PartitionSpec as P

HEAD_DIM = 64
BLOCK = 128
LANES = 128
MIB = 2**20

epsilon = 1e-06


f32 = jnp.float32
bf16 = jnp.bfloat16


def dot(x, y, dims=((1,), (0,))):
    return lax.dot_general(x, y, (dims, ((), ())), preferred_element_type=f32)


NT = ((1,), (1,))
TN = ((0,), (0,))


def tiles(ref):
    return ref.shape[1] // LANES


def tile(ref, t):
    return ref[:, t * LANES : (t + 1) * LANES]


def lane_is_low(shape):
    return lax.broadcasted_iota(jnp.int32, shape, 1) < HEAD_DIM


def by_head(x):
    low = lane_is_low(x.shape)
    zero = jnp.zeros_like(x)
    return jnp.where(low, x, zero), jnp.where(low, zero, x)


def pack_state(product):
    low = lane_is_low((HEAD_DIM, LANES))
    return jnp.where(low, product[:HEAD_DIM], product[HEAD_DIM:])


def unpack_state(state):
    low = lane_is_low(state.shape)
    zero = jnp.zeros_like(state)
    return jnp.concatenate([jnp.where(low, state, zero), jnp.where(low, zero, state)], axis=0)


def states_kernel(q_hbm, k_hbm, v_hbm, g_hbm, kv_ref, qg_ref, q_ref, k_ref, v_ref, g_ref, sems):
    sources = (k_hbm, v_hbm, g_hbm, q_hbm)
    targets = (k_ref, v_ref, g_ref, q_ref)
    copies = [
        pltpu.make_async_copy(source, target, sems.at[i])
        for i, (source, target) in enumerate(zip(sources, targets))
    ]
    for copy in copies:
        copy.start()
    for copy in copies:
        copy.wait()
    for t in range(tiles(q_ref)):
        rows = slice(t * HEAD_DIM, (t + 1) * HEAD_DIM)
        kv_ref[rows] = pack_state(dot(tile(k_ref, t), tile(v_ref, t), TN))
        qg_ref[rows] = pack_state(dot(tile(g_ref, t), tile(q_ref, t), TN))


def block_kernel(
    factor, q_ref, k_ref, v_ref, g_ref, gain_ref, out_ref, dq_ref, dk_ref, dv_ref, row_ref
):
    row_ref[...] = gain_ref[...]
    row = lax.broadcasted_iota(jnp.int32, (BLOCK, BLOCK), 0)
    column = lax.broadcasted_iota(jnp.int32, (BLOCK, BLOCK), 1)
    causal = row >= column
    for t in range(tiles(q_ref)):
        q, k, v, g = (tile(ref, t) for ref in (q_ref, k_ref, v_ref, g_ref))
        cols = slice(t * LANES, (t + 1) * LANES)
        out = dq = dk = dv = None
        for qh, gh, kh, vh in zip(by_head(q), by_head(g), by_head(k), by_head(v)):
            weights = (factor * jnp.where(causal, dot(qh, k, NT), 0.0)).astype(bf16)
            dweights = (factor * jnp.where(causal, dot(gh, v, NT), 0.0)).astype(bf16)
            parts = (dot(weights, vh), dot(dweights, kh), dot(dweights, qh, TN), dot(weights, gh, TN))
            if out is None:
                out, dq, dk, dv = parts
            else:
                out, dq, dk, dv = (x + y for x, y in zip((out, dq, dk, dv), parts))
        out_ref[:, cols] = out
        dq_ref[:, cols] = dq
        dk_ref[:, cols] = dk
        dv_ref[:, cols] = dv


def output_kernel(factor, q_ref, part_ref, kv_ref, out_ref, squares_ref):
    total = None
    for t in range(tiles(q_ref)):
        cols = slice(t * LANES, (t + 1) * LANES)
        state = unpack_state((factor * kv_ref[t * HEAD_DIM : (t + 1) * HEAD_DIM]).astype(bf16))
        out = part_ref[:, cols] + dot(tile(q_ref, t), state)
        out_ref[:, cols] = out
        square = out * out
        total = square if total is None else total + square
    squares_ref[...] = jnp.sum(total.T, axis=0, keepdims=True)


def grads_kernel(
    factor, k_ref, v_ref, g_ref, dq_part, dk_part, dv_part, kv_ref, qg_ref, dq_ref, dk_ref, dv_ref
):
    for t in range(tiles(k_ref)):
        cols = slice(t * LANES, (t + 1) * LANES)
        rows = slice(t * HEAD_DIM, (t + 1) * HEAD_DIM)
        state = unpack_state((factor * kv_ref[rows]).astype(bf16))
        grad_state = unpack_state((factor * qg_ref[rows]).astype(bf16))
        dq_ref[:, cols] = (dq_part[:, cols] + dot(tile(g_ref, t), state, NT)).astype(bf16)
        dk_ref[:, cols] = (dk_part[:, cols] + dot(tile(v_ref, t), grad_state)).astype(bf16)
        dv_ref[:, cols] = (dv_part[:, cols] + dot(tile(k_ref, t), grad_state, NT)).astype(bf16)


def norm_kernel(width, out_ref, squares_ref, gain_ref, normed_ref):
    total = jnp.sum(squares_ref[...], axis=0, keepdims=True)
    scale = lax.rsqrt(total / width + epsilon)
    scale = jnp.broadcast_to(scale, (LANES, scale.shape[1])).T
    for t in range(tiles(out_ref)):
        cols = slice(t * LANES, (t + 1) * LANES)
        normed_ref[:, cols] = (out_ref[:, cols] * scale * gain_ref[:, cols]).astype(bf16)


def call(kernel, outs, args, flops, vmem=16 * MIB, **spec):
    moved = sum(math.prod(a.shape) * jnp.dtype(a.dtype).itemsize for a in (*args, *outs))
    whole = pl.BlockSpec(memory_space=pltpu.VMEM)
    single = len(outs) == 1
    return pl.pallas_call(
        kernel,
        out_shape=outs[0] if single else tuple(outs),
        in_specs=[pl.BlockSpec(memory_space=spec.pop("inputs_at", pltpu.VMEM))] * len(args),
        out_specs=whole if single else tuple([whole] * len(outs)),
        compiler_params=pltpu.CompilerParams(vmem_limit_bytes=vmem),
        cost_estimate=pl.CostEstimate(flops=flops, bytes_accessed=moved, transcendentals=0),
        **spec,
    )(*args)


def swap(x, axis, distance):
    size = lax.axis_size(axis)
    return lax.ppermute(x, axis, [(i, i ^ distance) for i in range(size)])


def halves(x, odd):
    mid = x.shape[0] // 2
    low, high = x[:mid], x[mid:]
    return jnp.where(odd, high, low), jnp.where(odd, low, high)


def join(mine, other, odd):
    return jnp.concatenate([jnp.where(odd, other, mine), jnp.where(odd, mine, other)], axis=0)


def scan_states(kv, qg, axis):
    count = lax.axis_size(axis)
    index = lax.axis_index(axis)
    bit = lambda d: (index & d) != 0
    zero = jnp.zeros_like(kv)
    top = count // 2
    if count & (count - 1):
        position = jnp.arange(count)[:, None, None]
        every_kv = lax.all_gather(kv, axis)
        every_qg = lax.all_gather(qg, axis)
        return (
            jnp.sum(jnp.where(position < index, every_kv, 0.0), axis=0),
            jnp.sum(jnp.where(position > index, every_qg, 0.0), axis=0),
        )
    if count < 4:
        before, after, total_kv, total_qg = zero, zero, kv, qg
        distance = 1
        while distance < count:
            got_kv, got_qg = swap(total_kv, axis, distance), swap(total_qg, axis, distance)
            before = before + jnp.where(bit(distance), got_kv, 0.0)
            after = after + jnp.where(bit(distance), 0.0, got_qg)
            total_kv, total_qg = total_kv + got_kv, total_qg + got_qg
            distance *= 2
        return before, after
    odd, upper = bit(1), bit(top)
    a, b = jnp.where(upper, qg, kv), jnp.where(upper, kv, qg)
    (a_mine, a_other), (b_mine, b_other) = halves(a, odd), halves(b, odd)
    mid = a_mine.shape[0]
    a_enters = lambda d: bit(d) != upper
    b_enters = lambda d: bit(d) == upper
    got = swap(jnp.concatenate([a_other, b_other], axis=0), axis, 1)
    a1, b1 = got[:mid], got[mid:]
    a_total, b_total = a_mine + a1, b_mine + b1
    a_sum = b_sum = jnp.zeros_like(a_mine)
    distance = 2
    while distance < top:
        got = swap(jnp.concatenate([a_total, b_total], axis=0), axis, distance)
        a_sum = a_sum + jnp.where(a_enters(distance), got[:mid], 0.0)
        b_sum = b_sum + jnp.where(b_enters(distance), got[mid:], 0.0)
        a_total, b_total = a_total + got[:mid], b_total + got[mid:]
        distance *= 2
    t_other = swap(a_total, axis, top | 1)
    t_mine = swap(a_total, axis, top)
    a_out = a_sum + jnp.where(a_enters(1), 0.0, a_mine)
    b_out = b_sum + jnp.where(b_enters(1), 0.0, b_mine)
    got = swap(jnp.concatenate([a_out, b_out], axis=0), axis, 1)
    a_own = a_sum + jnp.where(a_enters(1), a1, 0.0)
    b_own = b_sum + jnp.where(b_enters(1), b1, 0.0) + t_mine
    a_all = join(a_own, got[:mid], odd)
    b_all = join(b_own, got[mid:] + t_other, odd)
    return jnp.where(upper, b_all, a_all), jnp.where(upper, a_all, b_all)


def all_shares(row, axis):
    count = lax.axis_size(axis)
    if count & (count - 1):
        return lax.psum(row, axis)
    if count > 4:
        distance = 1
        while distance < count:
            row = row + swap(row, axis, distance)
            distance *= 2
        return row
    return jnp.concatenate([row] + [swap(row, axis, d) for d in range(1, count)], axis=0)


def body(queries, keys, values, d_out, gain):
    length, width = queries.shape
    factor = 1.0 / math.sqrt(HEAD_DIM * length * lax.axis_size("seq"))
    packed = jax.ShapeDtypeStruct((width // LANES * HEAD_DIM, LANES), f32)
    wide = jax.ShapeDtypeStruct((length, width), f32)
    narrow = jax.ShapeDtypeStruct((length, width), bf16)
    inputs = (queries, keys, values, d_out)
    kv, qg = call(
        states_kernel,
        [packed] * 2,
        inputs,
        4 * length * LANES * width,
        vmem=64 * MIB - 10600 * 1024,
        inputs_at=pltpu.HBM,
        scratch_shapes=[pltpu.VMEM((length, width), bf16)] * 4 + [pltpu.SemaphoreType.DMA((4,))],
    )
    out_part, dq_part, dk_part, dv_part, gain_row = call(
        functools.partial(block_kernel, factor),
        [wide] * 4 + [jax.ShapeDtypeStruct((1, width), f32)],
        (*inputs, gain[None]),
        24 * length * LANES * width,
    )
    before, after = scan_states(kv, qg, "seq")
    out, squares = call(
        functools.partial(output_kernel, factor),
        [wide, jax.ShapeDtypeStruct((1, length), f32)],
        (queries, out_part, before),
        2 * length * LANES * width,
    )
    shares = all_shares(squares, "head")
    dq, dk, dv = call(
        functools.partial(grads_kernel, factor),
        [narrow] * 3,
        (keys, values, d_out, dq_part, dk_part, dv_part, before, after),
        6 * length * LANES * width,
    )
    normed = call(
        functools.partial(norm_kernel, width * lax.axis_size("head")),
        [narrow],
        (out, shares, gain_row),
        2 * length * width,
    )
    return normed, dq, dk, dv


def solution(mesh):
    placed = (P("seq", "head"), P("seq", "head"), P("seq", "head"), P("seq", "head"), P("head"))

    return jax.shard_map(
        body,
        mesh=mesh,
        in_specs=placed,
        out_specs=(P("seq", "head"), P("seq", "head"), P("seq", "head"), P("seq", "head")),
        check_vma=False,
    )
```

```python
import functools
import math

import jax
import jax.numpy as jnp
from jax import lax
from jax.experimental import pallas as pl
from jax.experimental.pallas import tpu as pltpu
from jax.sharding import PartitionSpec as P


HEAD_DIM = 64
BLOCK = 128
LANES = 128
MIB = 2**20

epsilon = 1e-06


f32 = jnp.float32
bf16 = jnp.bfloat16


def dot(x, y, dims=((1,), (0,))):
    return lax.dot_general(x, y, (dims, ((), ())), preferred_element_type=f32)


NT = ((1,), (1,))
TN = ((0,), (0,))


def tiles(ref):
    return ref.shape[1] // LANES


def tile(ref, t):
    return ref[:, t * LANES : (t + 1) * LANES]


def lane_is_low(shape):
    return lax.broadcasted_iota(jnp.int32, shape, 1) < HEAD_DIM


def by_head(x):
    low = lane_is_low(x.shape)
    zero = jnp.zeros_like(x)
    return jnp.where(low, x, zero), jnp.where(low, zero, x)


def pack_state(product):
    low = lane_is_low((HEAD_DIM, LANES))
    return jnp.where(low, product[:HEAD_DIM], product[HEAD_DIM:])


def unpack_state(state):
    low = lane_is_low(state.shape)
    zero = jnp.zeros_like(state)
    return jnp.concatenate([jnp.where(low, state, zero), jnp.where(low, zero, state)], axis=0)


def states_kernel(q_hbm, k_hbm, v_hbm, g_hbm, kv_ref, qg_ref, q_ref, k_ref, v_ref, g_ref, sems):
    sources = (k_hbm, v_hbm, g_hbm, q_hbm)
    targets = (k_ref, v_ref, g_ref, q_ref)
    copies = [
        pltpu.make_async_copy(source, target, sems.at[i])
        for i, (source, target) in enumerate(zip(sources, targets))
    ]
    for copy in copies:
        copy.start()
    for copy in copies:
        copy.wait()
    for t in range(tiles(q_ref)):
        rows = slice(t * HEAD_DIM, (t + 1) * HEAD_DIM)
        kv_ref[rows] = pack_state(dot(tile(k_ref, t), tile(v_ref, t), TN))
        qg_ref[rows] = pack_state(dot(tile(g_ref, t), tile(q_ref, t), TN))


def block_kernel(
    factor, q_ref, k_ref, v_ref, g_ref, gain_ref, out_ref, dq_ref, dk_ref, dv_ref, row_ref
):
    row_ref[...] = gain_ref[...]
    row = lax.broadcasted_iota(jnp.int32, (BLOCK, BLOCK), 0)
    column = lax.broadcasted_iota(jnp.int32, (BLOCK, BLOCK), 1)
    causal = row >= column
    for t in range(tiles(q_ref)):
        q, k, v, g = (tile(ref, t) for ref in (q_ref, k_ref, v_ref, g_ref))
        cols = slice(t * LANES, (t + 1) * LANES)
        out = dq = dk = dv = None
        for qh, gh, kh, vh in zip(by_head(q), by_head(g), by_head(k), by_head(v)):
            weights = (factor * jnp.where(causal, dot(qh, k, NT), 0.0)).astype(bf16)
            dweights = (factor * jnp.where(causal, dot(gh, v, NT), 0.0)).astype(bf16)
            parts = (dot(weights, vh), dot(dweights, kh), dot(dweights, qh, TN), dot(weights, gh, TN))
            if out is None:
                out, dq, dk, dv = parts
            else:
                out, dq, dk, dv = (x + y for x, y in zip((out, dq, dk, dv), parts))
        out_ref[:, cols] = out
        dq_ref[:, cols] = dq
        dk_ref[:, cols] = dk
        dv_ref[:, cols] = dv


def output_kernel(factor, q_ref, part_ref, kv_ref, out_ref, squares_ref):
    total = None
    for t in range(tiles(q_ref)):
        cols = slice(t * LANES, (t + 1) * LANES)
        state = unpack_state((factor * kv_ref[t * HEAD_DIM : (t + 1) * HEAD_DIM]).astype(bf16))
        out = part_ref[:, cols] + dot(tile(q_ref, t), state)
        out_ref[:, cols] = out
        square = out * out
        total = square if total is None else total + square
    squares_ref[...] = jnp.sum(total.T, axis=0, keepdims=True)


def grads_kernel(
    factor, k_ref, v_ref, g_ref, dq_part, dk_part, dv_part, kv_ref, qg_ref, dq_ref, dk_ref, dv_ref
):
    for t in range(tiles(k_ref)):
        cols = slice(t * LANES, (t + 1) * LANES)
        rows = slice(t * HEAD_DIM, (t + 1) * HEAD_DIM)
        state = unpack_state((factor * kv_ref[rows]).astype(bf16))
        grad_state = unpack_state((factor * qg_ref[rows]).astype(bf16))
        dq_ref[:, cols] = (dq_part[:, cols] + dot(tile(g_ref, t), state, NT)).astype(bf16)
        dk_ref[:, cols] = (dk_part[:, cols] + dot(tile(v_ref, t), grad_state)).astype(bf16)
        dv_ref[:, cols] = (dv_part[:, cols] + dot(tile(k_ref, t), grad_state, NT)).astype(bf16)


def norm_kernel(width, out_ref, squares_ref, gain_ref, normed_ref):
    total = jnp.sum(squares_ref[...], axis=0, keepdims=True)
    scale = lax.rsqrt(total / width + epsilon)
    scale = jnp.broadcast_to(scale, (LANES, scale.shape[1])).T
    for t in range(tiles(out_ref)):
        cols = slice(t * LANES, (t + 1) * LANES)
        normed_ref[:, cols] = (out_ref[:, cols] * scale * gain_ref[:, cols]).astype(bf16)


def call(kernel, outs, args, flops, vmem=16 * MIB, **spec):
    moved = sum(math.prod(a.shape) * jnp.dtype(a.dtype).itemsize for a in (*args, *outs))
    whole = pl.BlockSpec(memory_space=pltpu.VMEM)
    single = len(outs) == 1
    return pl.pallas_call(
        kernel,
        out_shape=outs[0] if single else tuple(outs),
        in_specs=[pl.BlockSpec(memory_space=spec.pop("inputs_at", pltpu.VMEM))] * len(args),
        out_specs=whole if single else tuple([whole] * len(outs)),
        compiler_params=pltpu.CompilerParams(vmem_limit_bytes=vmem),
        cost_estimate=pl.CostEstimate(flops=flops, bytes_accessed=moved, transcendentals=0),
        **spec,
    )(*args)


def swap(x, axis, distance):
    size = lax.axis_size(axis)
    return lax.ppermute(x, axis, [(i, i ^ distance) for i in range(size)])


def halves(x, odd):
    mid = x.shape[0] // 2
    low, high = x[:mid], x[mid:]
    return jnp.where(odd, high, low), jnp.where(odd, low, high)


def join(mine, other, odd):
    return jnp.concatenate([jnp.where(odd, other, mine), jnp.where(odd, mine, other)], axis=0)


def scan_states(kv, qg, axis):
    count = lax.axis_size(axis)
    index = lax.axis_index(axis)
    bit = lambda d: (index & d) != 0
    zero = jnp.zeros_like(kv)
    top = count // 2
    if count & (count - 1):
        position = jnp.arange(count)[:, None, None]
        every_kv = lax.all_gather(kv, axis)
        every_qg = lax.all_gather(qg, axis)
        return (
            jnp.sum(jnp.where(position < index, every_kv, 0.0), axis=0),
            jnp.sum(jnp.where(position > index, every_qg, 0.0), axis=0),
        )
    if count < 4:
        before, after, total_kv, total_qg = zero, zero, kv, qg
        distance = 1
        while distance < count:
            got_kv, got_qg = swap(total_kv, axis, distance), swap(total_qg, axis, distance)
            before = before + jnp.where(bit(distance), got_kv, 0.0)
            after = after + jnp.where(bit(distance), 0.0, got_qg)
            total_kv, total_qg = total_kv + got_kv, total_qg + got_qg
            distance *= 2
        return before, after
    odd, upper = bit(1), bit(top)
    a, b = jnp.where(upper, qg, kv), jnp.where(upper, kv, qg)
    a_enters = lambda d: bit(d) != upper
    b_enters = lambda d: bit(d) == upper

    def send(x, distance):
        return swap(x, axis, distance)

    (a_mine, a_other), (b_mine, b_other) = halves(a, odd), halves(b, odd)
    a1 = send(a_other, 1)
    b1 = send(b_other, 1)
    a_total, b_total = a_mine + a1, b_mine + b1
    a_sum = b_sum = jnp.zeros_like(a_mine)
    distance = 2
    while distance < top:
        a_got = send(a_total, distance)
        b_got = send(b_total, distance)
        a_sum = a_sum + jnp.where(a_enters(distance), a_got, 0.0)
        b_sum = b_sum + jnp.where(b_enters(distance), b_got, 0.0)
        a_total, b_total = a_total + a_got, b_total + b_got
        distance *= 2
    t_other = send(a_total, top | 1)
    t_mine = send(a_total, top)
    a_out = a_sum + jnp.where(a_enters(1), 0.0, a_mine)
    b_out = b_sum + jnp.where(b_enters(1), 0.0, b_mine)
    got = send(jnp.concatenate([a_out, b_out], axis=0), 1)
    mid = a_mine.shape[0]
    a_own = a_sum + jnp.where(a_enters(1), a1, 0.0)
    b_own = b_sum + jnp.where(b_enters(1), b1, 0.0) + t_mine
    a_all = join(a_own, got[:mid], odd)
    b_all = join(b_own, got[mid:] + t_other, odd)
    return jnp.where(upper, b_all, a_all), jnp.where(upper, a_all, b_all)


def all_shares(row, axis):
    count = lax.axis_size(axis)
    if count & (count - 1):
        return lax.psum(row, axis)
    if count > 4:
        distance = 1
        while distance < count:
            row = row + swap(row, axis, distance)
            distance *= 2
        return row
    return jnp.concatenate([row] + [swap(row, axis, d) for d in range(1, count)], axis=0)


def body(queries, keys, values, d_out, gain):
    length, width = queries.shape
    factor = 1.0 / math.sqrt(HEAD_DIM * length * lax.axis_size("seq"))
    packed = jax.ShapeDtypeStruct((width // LANES * HEAD_DIM, LANES), f32)
    wide = jax.ShapeDtypeStruct((length, width), f32)
    narrow = jax.ShapeDtypeStruct((length, width), bf16)
    inputs = (queries, keys, values, d_out)
    kv, qg = call(
        states_kernel,
        [packed] * 2,
        inputs,
        4 * length * LANES * width,
        vmem=64 * MIB - 10600 * 1024,
        inputs_at=pltpu.HBM,
        scratch_shapes=[pltpu.VMEM((length, width), bf16)] * 4 + [pltpu.SemaphoreType.DMA((4,))],
    )
    out_part, dq_part, dk_part, dv_part, gain_row = call(
        functools.partial(block_kernel, factor),
        [wide] * 4 + [jax.ShapeDtypeStruct((1, width), f32)],
        (*inputs, gain[None]),
        24 * length * LANES * width,
    )
    before, after = scan_states(kv, qg, "seq")
    out, squares = call(
        functools.partial(output_kernel, factor),
        [wide, jax.ShapeDtypeStruct((1, length), f32)],
        (queries, out_part, before),
        2 * length * LANES * width,
    )
    shares = all_shares(squares, "head")
    dq, dk, dv = call(
        functools.partial(grads_kernel, factor),
        [narrow] * 3,
        (keys, values, d_out, dq_part, dk_part, dv_part, before, after),
        6 * length * LANES * width,
    )
    normed = call(
        functools.partial(norm_kernel, width * lax.axis_size("head")),
        [narrow],
        (out, shares, gain_row),
        2 * length * width,
    )
    return normed, dq, dk, dv


def solution(mesh):
    placed = (P("seq", "head"), P("seq", "head"), P("seq", "head"), P("seq", "head"), P("head"))

    return jax.shard_map(
        body,
        mesh=mesh,
        in_specs=placed,
        out_specs=(P("seq", "head"), P("seq", "head"), P("seq", "head"), P("seq", "head")),
        check_vma=False,
    )
```

```python
import functools
import math

import jax
import jax.numpy as jnp
from jax import lax
from jax.experimental import pallas as pl
from jax.experimental.pallas import tpu as pltpu
from jax.sharding import PartitionSpec as P


HEAD_DIM = 64
BLOCK = 128
LANES = 128
MIB = 2**20

epsilon = 1e-06


f32 = jnp.float32
bf16 = jnp.bfloat16


def dot(x, y, dims=((1,), (0,))):
    return lax.dot_general(x, y, (dims, ((), ())), preferred_element_type=f32)


NT = ((1,), (1,))
TN = ((0,), (0,))


def tiles(ref):
    return ref.shape[1] // LANES


def tile(ref, t):
    return ref[:, t * LANES : (t + 1) * LANES]


def lane_is_low(shape):
    return lax.broadcasted_iota(jnp.int32, shape, 1) < HEAD_DIM


def by_head(x):
    low = lane_is_low(x.shape)
    zero = jnp.zeros_like(x)
    return jnp.where(low, x, zero), jnp.where(low, zero, x)


def pack_state(product):
    low = lane_is_low((HEAD_DIM, LANES))
    return jnp.where(low, product[:HEAD_DIM], product[HEAD_DIM:])


def unpack_state(state):
    low = lane_is_low(state.shape)
    zero = jnp.zeros_like(state)
    return jnp.concatenate([jnp.where(low, state, zero), jnp.where(low, zero, state)], axis=0)


def states_kernel(q_hbm, k_hbm, v_hbm, g_hbm, kv_ref, qg_ref, q_ref, k_ref, v_ref, g_ref, sems):
    sources = (k_hbm, v_hbm, g_hbm, q_hbm)
    targets = (k_ref, v_ref, g_ref, q_ref)
    copies = [
        pltpu.make_async_copy(source, target, sems.at[i])
        for i, (source, target) in enumerate(zip(sources, targets))
    ]
    for copy in copies:
        copy.start()
    for copy in copies:
        copy.wait()
    for t in range(tiles(q_ref)):
        rows = slice(t * HEAD_DIM, (t + 1) * HEAD_DIM)
        kv_ref[rows] = pack_state(dot(tile(k_ref, t), tile(v_ref, t), TN))
        qg_ref[rows] = pack_state(dot(tile(g_ref, t), tile(q_ref, t), TN))


def block_kernel(
    factor, q_ref, k_ref, v_ref, g_ref, gain_ref, out_ref, dq_ref, dk_ref, dv_ref, row_ref
):
    row_ref[...] = gain_ref[...]
    row = lax.broadcasted_iota(jnp.int32, (BLOCK, BLOCK), 0)
    column = lax.broadcasted_iota(jnp.int32, (BLOCK, BLOCK), 1)
    causal = row >= column
    for t in range(tiles(q_ref)):
        q, k, v, g = (tile(ref, t) for ref in (q_ref, k_ref, v_ref, g_ref))
        cols = slice(t * LANES, (t + 1) * LANES)
        out = dq = dk = dv = None
        for qh, gh, kh, vh in zip(by_head(q), by_head(g), by_head(k), by_head(v)):
            weights = (factor * jnp.where(causal, dot(qh, k, NT), 0.0)).astype(bf16)
            dweights = (factor * jnp.where(causal, dot(gh, v, NT), 0.0)).astype(bf16)
            parts = (dot(weights, vh), dot(dweights, kh), dot(dweights, qh, TN), dot(weights, gh, TN))
            if out is None:
                out, dq, dk, dv = parts
            else:
                out, dq, dk, dv = (x + y for x, y in zip((out, dq, dk, dv), parts))
        out_ref[:, cols] = out
        dq_ref[:, cols] = dq
        dk_ref[:, cols] = dk
        dv_ref[:, cols] = dv


def output_kernel(factor, q_ref, part_ref, kv_ref, out_ref, squares_ref):
    total = None
    for t in range(tiles(q_ref)):
        cols = slice(t * LANES, (t + 1) * LANES)
        state = unpack_state((factor * kv_ref[t * HEAD_DIM : (t + 1) * HEAD_DIM]).astype(bf16))
        out = part_ref[:, cols] + dot(tile(q_ref, t), state)
        out_ref[:, cols] = out
        square = out * out
        total = square if total is None else total + square
    squares_ref[...] = jnp.sum(total.T, axis=0, keepdims=True)


def grads_kernel(
    factor, k_ref, v_ref, g_ref, dq_part, dk_part, dv_part, kv_ref, qg_ref, dq_ref, dk_ref, dv_ref
):
    for t in range(tiles(k_ref)):
        cols = slice(t * LANES, (t + 1) * LANES)
        rows = slice(t * HEAD_DIM, (t + 1) * HEAD_DIM)
        state = unpack_state((factor * kv_ref[rows]).astype(bf16))
        grad_state = unpack_state((factor * qg_ref[rows]).astype(bf16))
        dq_ref[:, cols] = (dq_part[:, cols] + dot(tile(g_ref, t), state, NT)).astype(bf16)
        dk_ref[:, cols] = (dk_part[:, cols] + dot(tile(v_ref, t), grad_state)).astype(bf16)
        dv_ref[:, cols] = (dv_part[:, cols] + dot(tile(k_ref, t), grad_state, NT)).astype(bf16)


def norm_kernel(width, out_ref, squares_ref, gain_ref, normed_ref):
    total = jnp.sum(squares_ref[...], axis=0, keepdims=True)
    scale = lax.rsqrt(total / width + epsilon)
    scale = jnp.broadcast_to(scale, (LANES, scale.shape[1])).T
    for t in range(tiles(out_ref)):
        cols = slice(t * LANES, (t + 1) * LANES)
        normed_ref[:, cols] = (out_ref[:, cols] * scale * gain_ref[:, cols]).astype(bf16)


def call(kernel, outs, args, flops, vmem=16 * MIB, **spec):
    moved = sum(math.prod(a.shape) * jnp.dtype(a.dtype).itemsize for a in (*args, *outs))
    whole = pl.BlockSpec(memory_space=pltpu.VMEM)
    single = len(outs) == 1
    return pl.pallas_call(
        kernel,
        out_shape=outs[0] if single else tuple(outs),
        in_specs=[pl.BlockSpec(memory_space=spec.pop("inputs_at", pltpu.VMEM))] * len(args),
        out_specs=whole if single else tuple([whole] * len(outs)),
        compiler_params=pltpu.CompilerParams(vmem_limit_bytes=vmem),
        cost_estimate=pl.CostEstimate(flops=flops, bytes_accessed=moved, transcendentals=0),
        **spec,
    )(*args)


def swap(x, axis, distance):
    size = lax.axis_size(axis)
    return lax.ppermute(x, axis, [(i, i ^ distance) for i in range(size)])


def halves(x, odd):
    mid = x.shape[0] // 2
    low, high = x[:mid], x[mid:]
    return jnp.where(odd, high, low), jnp.where(odd, low, high)


def join(mine, other, odd):
    return jnp.concatenate([jnp.where(odd, other, mine), jnp.where(odd, mine, other)], axis=0)


def scan_states(kv, qg, axis):
    count = lax.axis_size(axis)
    index = lax.axis_index(axis)
    bit = lambda d: (index & d) != 0
    zero = jnp.zeros_like(kv)
    top = count // 2
    if count & (count - 1):
        position = jnp.arange(count)[:, None, None]
        every_kv = lax.all_gather(kv, axis)
        every_qg = lax.all_gather(qg, axis)
        return (
            jnp.sum(jnp.where(position < index, every_kv, 0.0), axis=0),
            jnp.sum(jnp.where(position > index, every_qg, 0.0), axis=0),
        )
    if count < 4:
        before, after, total_kv, total_qg = zero, zero, kv, qg
        distance = 1
        while distance < count:
            got_kv, got_qg = swap(total_kv, axis, distance), swap(total_qg, axis, distance)
            before = before + jnp.where(bit(distance), got_kv, 0.0)
            after = after + jnp.where(bit(distance), 0.0, got_qg)
            total_kv, total_qg = total_kv + got_kv, total_qg + got_qg
            distance *= 2
        return before, after
    odd, upper = bit(1), bit(top)
    a, b = jnp.where(upper, qg, kv), jnp.where(upper, kv, qg)
    a_enters = lambda d: bit(d) != upper
    b_enters = lambda d: bit(d) == upper

    def send(x, distance):
        return swap(x, axis, distance)

    a_mine, a_other = halves(a, odd)
    a3 = send(a_other, 3)
    a2 = send(a_mine, 2)
    a1 = send(a_other, 1)
    b1 = send(b, 1)
    a_pair = a2 + a3
    a_sum = jnp.where(a_enters(2), a_pair, 0.0)
    a_total = a_mine + a1 + a_pair
    b_total = b + b1
    distance = 4
    while distance < top:
        a_got = send(a_total, distance)
        a_sum = a_sum + jnp.where(a_enters(distance), a_got, 0.0)
        a_total = a_total + a_got
        distance *= 2
    t_other = send(a_total, top | 1)
    t_mine = send(a_total, top)
    distance, b_parts = 2, []
    while distance < top:
        b_parts.append(send(b_total, distance))
        b_total = b_total + b_parts[-1]
        distance *= 2
    got = send(a_sum + jnp.where(a_enters(1), 0.0, a_mine), 1)
    a_sum, a1, got, b1, b_parts, t_mine, t_other = lax.optimization_barrier(
        (a_sum, a1, got, b1, b_parts, t_mine, t_other)
    )
    a_all = join(a_sum + jnp.where(a_enters(1), a1, 0.0), got, odd)
    b_all = join(t_mine, t_other, odd) + jnp.where(b_enters(1), b1, 0.0)
    for i, part in enumerate(b_parts):
        b_all = b_all + jnp.where(b_enters(2 << i), part, 0.0)
    return jnp.where(upper, b_all, a_all), jnp.where(upper, a_all, b_all)


def all_shares(row, axis):
    count = lax.axis_size(axis)
    if count & (count - 1):
        return lax.psum(row, axis)
    if count > 4:
        distance = 1
        while distance < count:
            row = row + swap(row, axis, distance)
            distance *= 2
        return row
    rows = [row]
    for distance in range(count - 1, 0, -1):
        rows.append(swap(row, axis, distance))
    return jnp.concatenate(rows, axis=0)


def body(queries, keys, values, d_out, gain):
    length, width = queries.shape
    factor = 1.0 / math.sqrt(HEAD_DIM * length * lax.axis_size("seq"))
    packed = jax.ShapeDtypeStruct((width // LANES * HEAD_DIM, LANES), f32)
    wide = jax.ShapeDtypeStruct((length, width), f32)
    narrow = jax.ShapeDtypeStruct((length, width), bf16)
    inputs = (queries, keys, values, d_out)
    kv, qg = call(
        states_kernel,
        [packed] * 2,
        inputs,
        4 * length * LANES * width,
        vmem=64 * MIB - 10600 * 1024,
        inputs_at=pltpu.HBM,
        scratch_shapes=[pltpu.VMEM((length, width), bf16)] * 4 + [pltpu.SemaphoreType.DMA((4,))],
    )
    out_part, dq_part, dk_part, dv_part, gain_row = call(
        functools.partial(block_kernel, factor),
        [wide] * 4 + [jax.ShapeDtypeStruct((1, width), f32)],
        (*inputs, gain[None]),
        24 * length * LANES * width,
    )
    before, after = scan_states(kv, qg, "seq")
    out, squares = call(
        functools.partial(output_kernel, factor),
        [wide, jax.ShapeDtypeStruct((1, length), f32)],
        (queries, out_part, before),
        2 * length * LANES * width,
    )
    shares = all_shares(squares, "head")
    dq, dk, dv = call(
        functools.partial(grads_kernel, factor),
        [narrow] * 3,
        (keys, values, d_out, dq_part, dk_part, dv_part, before, after),
        6 * length * LANES * width,
    )
    normed = call(
        functools.partial(norm_kernel, width * lax.axis_size("head")),
        [narrow],
        (out, shares, gain_row),
        2 * length * width,
    )
    return normed, dq, dk, dv


def solution(mesh):
    placed = (P("seq", "head"), P("seq", "head"), P("seq", "head"), P("seq", "head"), P("head"))

    return jax.shard_map(
        body,
        mesh=mesh,
        in_specs=placed,
        out_specs=(P("seq", "head"), P("seq", "head"), P("seq", "head"), P("seq", "head")),
        check_vma=False,
    )
```

```python
import functools
import math

import jax
import jax.numpy as jnp
from jax import lax
from jax.experimental import pallas as pl
from jax.experimental.pallas import tpu as pltpu
from jax.sharding import PartitionSpec as P


HEAD_DIM = 64
BLOCK = 128
LANES = 128
MIB = 2**20

epsilon = 1e-06


f32 = jnp.float32
bf16 = jnp.bfloat16


def dot(x, y, dims=((1,), (0,))):
    return lax.dot_general(x, y, (dims, ((), ())), preferred_element_type=f32)


NT = ((1,), (1,))
TN = ((0,), (0,))


def tiles(ref):
    return ref.shape[1] // LANES


def tile(ref, t):
    return ref[:, t * LANES : (t + 1) * LANES]


def lane_is_low(shape):
    return lax.broadcasted_iota(jnp.int32, shape, 1) < HEAD_DIM


def by_head(x):
    low = lane_is_low(x.shape)
    zero = jnp.zeros_like(x)
    return jnp.where(low, x, zero), jnp.where(low, zero, x)


def pack_state(product):
    low = lane_is_low((HEAD_DIM, LANES))
    return jnp.where(low, product[:HEAD_DIM], product[HEAD_DIM:])


def unpack_state(state):
    low = lane_is_low(state.shape)
    zero = jnp.zeros_like(state)
    return jnp.concatenate([jnp.where(low, state, zero), jnp.where(low, zero, state)], axis=0)


def states_kernel(q_hbm, k_hbm, v_hbm, g_hbm, kv_ref, qg_ref, q_ref, k_ref, v_ref, g_ref, sems):
    sources = (k_hbm, v_hbm, g_hbm, q_hbm)
    targets = (k_ref, v_ref, g_ref, q_ref)
    copies = [
        pltpu.make_async_copy(source, target, sems.at[i])
        for i, (source, target) in enumerate(zip(sources, targets))
    ]
    for copy in copies:
        copy.start()
    for copy in copies:
        copy.wait()
    for t in range(tiles(q_ref)):
        rows = slice(t * HEAD_DIM, (t + 1) * HEAD_DIM)
        kv_ref[rows] = pack_state(dot(tile(k_ref, t), tile(v_ref, t), TN))
        qg_ref[rows] = pack_state(dot(tile(g_ref, t), tile(q_ref, t), TN))


def block_kernel(
    factor, q_ref, k_ref, v_ref, g_ref, gain_ref, out_ref, dq_ref, dk_ref, dv_ref, row_ref
):
    row_ref[...] = gain_ref[...]
    row = lax.broadcasted_iota(jnp.int32, (BLOCK, BLOCK), 0)
    column = lax.broadcasted_iota(jnp.int32, (BLOCK, BLOCK), 1)
    causal = row >= column
    for t in range(tiles(q_ref)):
        q, k, v, g = (tile(ref, t) for ref in (q_ref, k_ref, v_ref, g_ref))
        cols = slice(t * LANES, (t + 1) * LANES)
        out = dq = dk = dv = None
        for qh, gh, kh, vh in zip(by_head(q), by_head(g), by_head(k), by_head(v)):
            weights = (factor * jnp.where(causal, dot(qh, k, NT), 0.0)).astype(bf16)
            dweights = (factor * jnp.where(causal, dot(gh, v, NT), 0.0)).astype(bf16)
            parts = (dot(weights, vh), dot(dweights, kh), dot(dweights, qh, TN), dot(weights, gh, TN))
            if out is None:
                out, dq, dk, dv = parts
            else:
                out, dq, dk, dv = (x + y for x, y in zip((out, dq, dk, dv), parts))
        out_ref[:, cols] = out
        dq_ref[:, cols] = dq
        dk_ref[:, cols] = dk
        dv_ref[:, cols] = dv


def output_kernel(factor, q_ref, part_ref, kv_ref, out_ref, squares_ref):
    total = None
    for t in range(tiles(q_ref)):
        cols = slice(t * LANES, (t + 1) * LANES)
        state = unpack_state((factor * kv_ref[t * HEAD_DIM : (t + 1) * HEAD_DIM]).astype(bf16))
        out = part_ref[:, cols] + dot(tile(q_ref, t), state)
        out_ref[:, cols] = out
        square = out * out
        total = square if total is None else total + square
    squares_ref[...] = jnp.sum(total.T, axis=0, keepdims=True)


def grads_kernel(
    factor, k_ref, v_ref, g_ref, dq_part, dk_part, dv_part, kv_ref, qg_ref, dq_ref, dk_ref, dv_ref
):
    for t in range(tiles(k_ref)):
        cols = slice(t * LANES, (t + 1) * LANES)
        rows = slice(t * HEAD_DIM, (t + 1) * HEAD_DIM)
        state = unpack_state((factor * kv_ref[rows]).astype(bf16))
        grad_state = unpack_state((factor * qg_ref[rows]).astype(bf16))
        dq_ref[:, cols] = (dq_part[:, cols] + dot(tile(g_ref, t), state, NT)).astype(bf16)
        dk_ref[:, cols] = (dk_part[:, cols] + dot(tile(v_ref, t), grad_state)).astype(bf16)
        dv_ref[:, cols] = (dv_part[:, cols] + dot(tile(k_ref, t), grad_state, NT)).astype(bf16)


def norm_kernel(width, out_ref, squares_ref, gain_ref, normed_ref):
    total = jnp.sum(squares_ref[...], axis=0, keepdims=True)
    scale = lax.rsqrt(total / width + epsilon)
    scale = jnp.broadcast_to(scale, (LANES, scale.shape[1])).T
    for t in range(tiles(out_ref)):
        cols = slice(t * LANES, (t + 1) * LANES)
        normed_ref[:, cols] = (out_ref[:, cols] * scale * gain_ref[:, cols]).astype(bf16)


def call(kernel, outs, args, flops, vmem=16 * MIB, **spec):
    moved = sum(math.prod(a.shape) * jnp.dtype(a.dtype).itemsize for a in (*args, *outs))
    whole = pl.BlockSpec(memory_space=pltpu.VMEM)
    single = len(outs) == 1
    return pl.pallas_call(
        kernel,
        out_shape=outs[0] if single else tuple(outs),
        in_specs=[pl.BlockSpec(memory_space=spec.pop("inputs_at", pltpu.VMEM))] * len(args),
        out_specs=whole if single else tuple([whole] * len(outs)),
        compiler_params=pltpu.CompilerParams(vmem_limit_bytes=vmem),
        cost_estimate=pl.CostEstimate(flops=flops, bytes_accessed=moved, transcendentals=0),
        **spec,
    )(*args)


def swap(x, axis, distance):
    size = lax.axis_size(axis)
    return lax.ppermute(x, axis, [(i, i ^ distance) for i in range(size)])


def halves(x, odd):
    mid = x.shape[0] // 2
    low, high = x[:mid], x[mid:]
    return jnp.where(odd, high, low), jnp.where(odd, low, high)


def join(mine, other, odd):
    return jnp.concatenate([jnp.where(odd, other, mine), jnp.where(odd, mine, other)], axis=0)


def scan_states(kv, qg, axis):
    count = lax.axis_size(axis)
    index = lax.axis_index(axis)
    bit = lambda d: (index & d) != 0
    zero = jnp.zeros_like(kv)
    top = count // 2
    if count & (count - 1):
        position = jnp.arange(count)[:, None, None]
        every_kv = lax.all_gather(kv, axis)
        every_qg = lax.all_gather(qg, axis)
        return (
            jnp.sum(jnp.where(position < index, every_kv, 0.0), axis=0),
            jnp.sum(jnp.where(position > index, every_qg, 0.0), axis=0),
        )
    if count < 4:
        before, after, total_kv, total_qg = zero, zero, kv, qg
        distance = 1
        while distance < count:
            got_kv, got_qg = swap(total_kv, axis, distance), swap(total_qg, axis, distance)
            before = before + jnp.where(bit(distance), got_kv, 0.0)
            after = after + jnp.where(bit(distance), 0.0, got_qg)
            total_kv, total_qg = total_kv + got_kv, total_qg + got_qg
            distance *= 2
        return before, after
    odd, upper = bit(1), bit(top)
    a, b = jnp.where(upper, qg, kv), jnp.where(upper, kv, qg)
    a_enters = lambda d: bit(d) != upper
    b_enters = lambda d: bit(d) == upper

    def send(x, distance):
        return swap(x, axis, distance)

    (a_mine, a_other), (b_mine, b_other) = halves(a, odd), halves(b, odd)
    mid = a_mine.shape[0]
    a3 = send(a_other, 3)
    a2 = send(a_mine, 2)
    a1 = send(a_other, 1)
    b3 = send(b_other, 3)
    b2 = send(b_mine, 2)
    b1 = send(b_other, 1)
    a_pair = a2 + a3
    a_sum = jnp.where(a_enters(2), a_pair, 0.0)
    a_total = a_mine + a1 + a_pair
    distance, a_later = 4, []
    while distance < top:
        a_later.append(send(a_total, distance))
        a_sum = a_sum + jnp.where(a_enters(distance), a_later[-1], 0.0)
        a_total = a_total + a_later[-1]
        distance *= 2
    t_other = send(a_total, top | 1)
    t_mine = send(a_total, top)
    b_pair = b2 + b3
    b_sum = jnp.where(b_enters(2), b_pair, 0.0)
    b_total = b_mine + b1 + b_pair
    distance = 4
    while distance < top:
        b_got = send(b_total, distance)
        b_sum = b_sum + jnp.where(b_enters(distance), b_got, 0.0)
        b_total = b_total + b_got
        distance *= 2
    a_out = a_sum + jnp.where(a_enters(1), 0.0, a_mine)
    b_out = b_sum + jnp.where(b_enters(1), 0.0, b_mine)
    got = send(jnp.concatenate([a_out, b_out], axis=0), 1)
    a_sum, a1, b_sum, b1, got, t_mine, t_other = lax.optimization_barrier(
        (a_sum, a1, b_sum, b1, got, t_mine, t_other)
    )
    a_all = join(a_sum + jnp.where(a_enters(1), a1, 0.0), got[:mid], odd)
    b_all = join(b_sum + jnp.where(b_enters(1), b1, 0.0) + t_mine, got[mid:] + t_other, odd)
    return jnp.where(upper, b_all, a_all), jnp.where(upper, a_all, b_all)


def all_shares(row, axis):
    count = lax.axis_size(axis)
    if count & (count - 1):
        return lax.psum(row, axis)
    if count > 4:
        distance = 1
        while distance < count:
            row = row + swap(row, axis, distance)
            distance *= 2
        return row
    rows = [row]
    for distance in range(count - 1, 0, -1):
        rows.append(swap(row, axis, distance))
    return jnp.concatenate(rows, axis=0)


def body(queries, keys, values, d_out, gain):
    length, width = queries.shape
    factor = 1.0 / math.sqrt(HEAD_DIM * length * lax.axis_size("seq"))
    packed = jax.ShapeDtypeStruct((width // LANES * HEAD_DIM, LANES), f32)
    wide = jax.ShapeDtypeStruct((length, width), f32)
    narrow = jax.ShapeDtypeStruct((length, width), bf16)
    inputs = (queries, keys, values, d_out)
    kv, qg = call(
        states_kernel,
        [packed] * 2,
        inputs,
        4 * length * LANES * width,
        vmem=64 * MIB - 10600 * 1024,
        inputs_at=pltpu.HBM,
        scratch_shapes=[pltpu.VMEM((length, width), bf16)] * 4 + [pltpu.SemaphoreType.DMA((4,))],
    )
    out_part, dq_part, dk_part, dv_part, gain_row = call(
        functools.partial(block_kernel, factor),
        [wide] * 4 + [jax.ShapeDtypeStruct((1, width), f32)],
        (*inputs, gain[None]),
        24 * length * LANES * width,
    )
    before, after = scan_states(kv, qg, "seq")
    out, squares = call(
        functools.partial(output_kernel, factor),
        [wide, jax.ShapeDtypeStruct((1, length), f32)],
        (queries, out_part, before),
        2 * length * LANES * width,
    )
    shares = all_shares(squares, "head")
    dq, dk, dv = call(
        functools.partial(grads_kernel, factor),
        [narrow] * 3,
        (keys, values, d_out, dq_part, dk_part, dv_part, before, after),
        6 * length * LANES * width,
    )
    normed = call(
        functools.partial(norm_kernel, width * lax.axis_size("head")),
        [narrow],
        (out, shares, gain_row),
        2 * length * width,
    )
    return normed, dq, dk, dv


def solution(mesh):
    placed = (P("seq", "head"), P("seq", "head"), P("seq", "head"), P("seq", "head"), P("head"))

    return jax.shard_map(
        body,
        mesh=mesh,
        in_specs=placed,
        out_specs=(P("seq", "head"), P("seq", "head"), P("seq", "head"), P("seq", "head")),
        check_vma=False,
    )
```

```python
import functools
import math

import jax
import jax.numpy as jnp
from jax import lax
from jax.experimental import pallas as pl
from jax.experimental.pallas import tpu as pltpu
from jax.sharding import PartitionSpec as P


HEAD_DIM = 64
BLOCK = 128
LANES = 128
MIB = 2**20

epsilon = 1e-06


f32 = jnp.float32
bf16 = jnp.bfloat16


def dot(x, y, dims=((1,), (0,))):
    return lax.dot_general(x, y, (dims, ((), ())), preferred_element_type=f32)


NT = ((1,), (1,))
TN = ((0,), (0,))


def tiles(ref):
    return ref.shape[1] // LANES


def tile(ref, t):
    return ref[:, t * LANES : (t + 1) * LANES]


def lane_is_low(shape):
    return lax.broadcasted_iota(jnp.int32, shape, 1) < HEAD_DIM


def by_head(x):
    low = lane_is_low(x.shape)
    zero = jnp.zeros_like(x)
    return jnp.where(low, x, zero), jnp.where(low, zero, x)


def pack_state(product):
    low = lane_is_low((HEAD_DIM, LANES))
    return jnp.where(low, product[:HEAD_DIM], product[HEAD_DIM:])


def unpack_state(state):
    low = lane_is_low(state.shape)
    zero = jnp.zeros_like(state)
    return jnp.concatenate([jnp.where(low, state, zero), jnp.where(low, zero, state)], axis=0)


def states_kernel(q_hbm, k_hbm, v_hbm, g_hbm, kv_ref, qg_ref, left_ref, right_ref, sems):
    copies = start_loads(q_hbm, k_hbm, v_hbm, g_hbm, left_ref, right_ref, sems)
    for out_ref, pair in ((kv_ref, 0), (qg_ref, 1)):
        wait_loads(copies, pair)
        for t in range(out_ref.shape[0] // HEAD_DIM):
            lanes = slice(t * LANES, (t + 1) * LANES)
            rows = slice(t * HEAD_DIM, (t + 1) * HEAD_DIM)
            out_ref[rows] = pack_state(dot(left_ref[pair, :, lanes], right_ref[pair, :, lanes], TN))


def start_loads(q_hbm, k_hbm, v_hbm, g_hbm, left_ref, right_ref, sems):
    copies = []
    for pair, (left, right) in enumerate(((k_hbm, v_hbm), (g_hbm, q_hbm))):
        copies.append(
            (
                pltpu.make_async_copy(left, left_ref.at[pair], sems.at[pair, 0]),
                pltpu.make_async_copy(right, right_ref.at[pair], sems.at[pair, 1]),
            )
        )
    for copy in (*copies[0], *copies[1]):
        copy.start()
    return copies


def wait_loads(copies, pair):
    for copy in copies[pair]:
        copy.wait()


def place_on(axis):
    index = lax.axis_index(axis)
    return index // (lax.axis_size(axis) // 2), index % 2


def halves_kernel(axis, *refs):
    q_hbm, k_hbm, v_hbm, g_hbm, a_mine, a_other, b_mine, b_other, left_ref, right_ref, sems = refs
    copies = start_loads(q_hbm, k_hbm, v_hbm, g_hbm, left_ref, right_ref, sems)
    upper, odd = place_on(axis)
    count = left_ref.shape[2] // LANES // 2
    wait_loads(copies, 0)
    wait_loads(copies, 1)
    outs = ((a_mine, upper, odd), (a_other, upper, 1 - odd), (b_mine, 1 - upper, odd), (b_other, 1 - upper, 1 - odd))
    for out_ref, pair, half in outs:
        for t in range(count):
            lanes = pl.ds(pl.multiple_of((half * count + t) * LANES, LANES), LANES)
            rows = slice(t * HEAD_DIM, (t + 1) * HEAD_DIM)
            out_ref[rows] = pack_state(dot(left_ref[pair, :, lanes], right_ref[pair, :, lanes], TN))


def whole_states(pieces, axis):
    if len(pieces) == 2:
        return tuple(lambda t, ref=ref: ref[t * HEAD_DIM : (t + 1) * HEAD_DIM] for ref in pieces)
    a_sum, a1, b_sum, b1, got, t_mine, t_other = pieces
    upper, odd = place_on(axis)
    mid = a_sum.shape[0]
    count = mid // HEAD_DIM

    def part(t, is_a):
        start = t % count * HEAD_DIM
        rows = slice(start, start + HEAD_DIM)
        if is_a:
            mine = a_sum[rows] + jnp.where(odd != upper, a1[rows], 0.0)
            other = got[rows]
        else:
            mine = b_sum[rows] + jnp.where(odd == upper, b1[rows], 0.0) + t_mine[rows]
            other = got[mid + start : mid + start + HEAD_DIM] + t_other[rows]
        return jnp.where(odd == t // count, mine, other)

    def kv_of(t):
        return jnp.where(upper == 1, part(t, False), part(t, True))

    def qg_of(t):
        return jnp.where(upper == 1, part(t, True), part(t, False))

    return kv_of, qg_of


def block_kernel(
    factor, q_ref, k_ref, v_ref, g_ref, gain_ref, out_ref, dq_ref, dk_ref, dv_ref, row_ref
):
    row_ref[...] = gain_ref[...]
    row = lax.broadcasted_iota(jnp.int32, (BLOCK, BLOCK), 0)
    column = lax.broadcasted_iota(jnp.int32, (BLOCK, BLOCK), 1)
    causal = row >= column
    for t in range(tiles(q_ref)):
        q, k, v, g = (tile(ref, t) for ref in (q_ref, k_ref, v_ref, g_ref))
        cols = slice(t * LANES, (t + 1) * LANES)
        out = dq = dk = dv = None
        for qh, gh, kh, vh in zip(by_head(q), by_head(g), by_head(k), by_head(v)):
            weights = (factor * jnp.where(causal, dot(qh, k, NT), 0.0)).astype(bf16)
            dweights = (factor * jnp.where(causal, dot(gh, v, NT), 0.0)).astype(bf16)
            parts = (dot(weights, vh), dot(dweights, kh), dot(dweights, qh, TN), dot(weights, gh, TN))
            if out is None:
                out, dq, dk, dv = parts
            else:
                out, dq, dk, dv = (x + y for x, y in zip((out, dq, dk, dv), parts))
        out_ref[:, cols] = out
        dq_ref[:, cols] = dq
        dk_ref[:, cols] = dk
        dv_ref[:, cols] = dv


def output_kernel(factor, axis, q_ref, part_ref, *refs):
    *pieces, out_ref, squares_ref = refs
    kv_of, _ = whole_states(pieces, axis)
    total = None
    for t in range(tiles(q_ref)):
        cols = slice(t * LANES, (t + 1) * LANES)
        state = unpack_state((factor * kv_of(t)).astype(bf16))
        out = part_ref[:, cols] + dot(tile(q_ref, t), state)
        out_ref[:, cols] = out
        square = out * out
        total = square if total is None else total + square
    squares_ref[...] = jnp.sum(total.T, axis=0, keepdims=True)


def grads_kernel(factor, axis, k_ref, v_ref, g_ref, dq_part, dk_part, dv_part, *refs):
    *pieces, dq_ref, dk_ref, dv_ref = refs
    kv_of, qg_of = whole_states(pieces, axis)
    for t in range(tiles(k_ref)):
        cols = slice(t * LANES, (t + 1) * LANES)
        state = unpack_state((factor * kv_of(t)).astype(bf16))
        grad_state = unpack_state((factor * qg_of(t)).astype(bf16))
        dq_ref[:, cols] = (dq_part[:, cols] + dot(tile(g_ref, t), state, NT)).astype(bf16)
        dk_ref[:, cols] = (dk_part[:, cols] + dot(tile(v_ref, t), grad_state)).astype(bf16)
        dv_ref[:, cols] = (dv_part[:, cols] + dot(tile(k_ref, t), grad_state, NT)).astype(bf16)


def norm_kernel(width, out_ref, gain_ref, *refs):
    *shares, normed_ref = refs
    total = shares[0][...]
    for share in shares[1:]:
        total = total + share[...]
    scale = lax.rsqrt(total / width + epsilon)
    scale = jnp.broadcast_to(scale, (LANES, scale.shape[1])).T
    for t in range(tiles(out_ref)):
        cols = slice(t * LANES, (t + 1) * LANES)
        normed_ref[:, cols] = (out_ref[:, cols] * scale * gain_ref[:, cols]).astype(bf16)


def call(kernel, outs, args, flops, vmem=16 * MIB, **spec):
    moved = sum(math.prod(a.shape) * jnp.dtype(a.dtype).itemsize for a in (*args, *outs))
    whole = pl.BlockSpec(memory_space=pltpu.VMEM)
    single = len(outs) == 1
    return pl.pallas_call(
        kernel,
        out_shape=outs[0] if single else tuple(outs),
        in_specs=[pl.BlockSpec(memory_space=spec.pop("inputs_at", pltpu.VMEM))] * len(args),
        out_specs=whole if single else tuple([whole] * len(outs)),
        compiler_params=pltpu.CompilerParams(vmem_limit_bytes=vmem),
        cost_estimate=pl.CostEstimate(flops=flops, bytes_accessed=moved, transcendentals=0),
        **spec,
    )(*args)


def swap(x, axis, distance):
    size = lax.axis_size(axis)
    return lax.ppermute(x, axis, [(i, i ^ distance) for i in range(size)])


def scan_states(axis, states, halves):
    count = lax.axis_size(axis)
    index = lax.axis_index(axis)
    bit = lambda d: (index & d) != 0
    top = count // 2
    if count & (count - 1):
        kv, qg = states()
        position = jnp.arange(count)[:, None, None]
        every_kv = lax.all_gather(kv, axis)
        every_qg = lax.all_gather(qg, axis)
        return (
            jnp.sum(jnp.where(position < index, every_kv, 0.0), axis=0),
            jnp.sum(jnp.where(position > index, every_qg, 0.0), axis=0),
        )
    if count < 8:
        total_kv, total_qg = states()
        before, after = jnp.zeros_like(total_kv), jnp.zeros_like(total_qg)
        distance = 1
        while distance < count:
            got_kv, got_qg = swap(total_kv, axis, distance), swap(total_qg, axis, distance)
            before = before + jnp.where(bit(distance), got_kv, 0.0)
            after = after + jnp.where(bit(distance), 0.0, got_qg)
            total_kv, total_qg = total_kv + got_kv, total_qg + got_qg
            distance *= 2
        return before, after
    upper = bit(top)
    a_enters = lambda d: bit(d) != upper
    b_enters = lambda d: bit(d) == upper

    def send(x, distance):
        return swap(x, axis, distance)

    a_mine, a_other, b_mine, b_other = halves()
    a3 = send(a_other, 3)
    a2 = send(a_mine, 2)
    a1 = send(a_other, 1)
    b3 = send(b_other, 3)
    b2 = send(b_mine, 2)
    b1 = send(b_other, 1)
    a_pair, b_pair = a2 + a3, b2 + b3
    a_sum = jnp.where(a_enters(2), a_pair, 0.0)
    b_sum = jnp.where(b_enters(2), b_pair, 0.0)
    a_total, b_total = a_mine + a1 + a_pair, b_mine + b1 + b_pair
    distance = 4
    while distance < top:
        a_got, b_got = send(a_total, distance), send(b_total, distance)
        a_sum = a_sum + jnp.where(a_enters(distance), a_got, 0.0)
        b_sum = b_sum + jnp.where(b_enters(distance), b_got, 0.0)
        a_total, b_total = a_total + a_got, b_total + b_got
        distance *= 2
    t_other = send(a_total, top | 1)
    t_mine = send(a_total, top)
    a_out = a_sum + jnp.where(a_enters(1), 0.0, a_mine)
    b_out = b_sum + jnp.where(b_enters(1), 0.0, b_mine)
    got = send(jnp.concatenate([a_out, b_out], axis=0), 1)
    return a_sum, a1, b_sum, b1, got, t_mine, t_other


def all_shares(row, axis):
    count = lax.axis_size(axis)
    if count & (count - 1):
        return [lax.psum(row, axis)]
    if count > 4:
        distance = 1
        while distance < count:
            row = row + swap(row, axis, distance)
            distance *= 2
        return [row]
    rows = [row]
    for distance in range(count - 1, 0, -1):
        rows.append(swap(row, axis, distance))
    return rows


def body(queries, keys, values, d_out, gain):
    length, width = queries.shape
    factor = 1.0 / math.sqrt(HEAD_DIM * length * lax.axis_size("seq"))
    packed = jax.ShapeDtypeStruct((width // LANES * HEAD_DIM, LANES), f32)
    wide = jax.ShapeDtypeStruct((length, width), f32)
    narrow = jax.ShapeDtypeStruct((length, width), bf16)
    inputs = (queries, keys, values, d_out)
    half = jax.ShapeDtypeStruct((packed.shape[0] // 2, LANES), f32)

    def products(kernel, outs):
        return call(
            kernel,
            outs,
            inputs,
            4 * length * LANES * width,
            vmem=64 * MIB - 10600 * 1024,
            inputs_at=pltpu.HBM,
            scratch_shapes=[pltpu.VMEM((2, length, width), bf16)] * 2
            + [pltpu.SemaphoreType.DMA((2, 2))],
        )

    out_part, dq_part, dk_part, dv_part, gain_row = call(
        functools.partial(block_kernel, factor),
        [wide] * 4 + [jax.ShapeDtypeStruct((1, width), f32)],
        (*inputs, gain[None]),
        24 * length * LANES * width,
    )
    pieces = scan_states(
        "seq",
        lambda: products(states_kernel, [packed] * 2),
        lambda: products(functools.partial(halves_kernel, "seq"), [half] * 4),
    )
    out, squares = call(
        functools.partial(output_kernel, factor, "seq"),
        [wide, jax.ShapeDtypeStruct((1, length), f32)],
        (queries, out_part, *pieces),
        2 * length * LANES * width,
    )
    shares = all_shares(squares, "head")
    dq, dk, dv = call(
        functools.partial(grads_kernel, factor, "seq"),
        [narrow] * 3,
        (keys, values, d_out, dq_part, dk_part, dv_part, *pieces),
        6 * length * LANES * width,
    )
    normed = call(
        functools.partial(norm_kernel, width * lax.axis_size("head")),
        [narrow],
        (out, gain_row, *shares),
        2 * length * width,
    )
    return normed, dq, dk, dv


def solution(mesh):
    placed = (P("seq", "head"), P("seq", "head"), P("seq", "head"), P("seq", "head"), P("head"))

    return jax.shard_map(
        body,
        mesh=mesh,
        in_specs=placed,
        out_specs=(P("seq", "head"), P("seq", "head"), P("seq", "head"), P("seq", "head")),
        check_vma=False,
    )
```

```python
import functools
import math

import jax
import jax.numpy as jnp
from jax import lax
from jax.experimental import pallas as pl
from jax.experimental.pallas import tpu as pltpu
from jax.sharding import PartitionSpec as P


HEAD_DIM = 64
BLOCK = 128
LANES = 128
MIB = 2**20

epsilon = 1e-06


f32 = jnp.float32
bf16 = jnp.bfloat16


def dot(x, y, dims=((1,), (0,))):
    return lax.dot_general(x, y, (dims, ((), ())), preferred_element_type=f32)


NT = ((1,), (1,))
TN = ((0,), (0,))


def tiles(ref):
    return ref.shape[1] // LANES


def tile(ref, t):
    return ref[:, t * LANES : (t + 1) * LANES]


def lane_is_low(shape):
    return lax.broadcasted_iota(jnp.int32, shape, 1) < HEAD_DIM


def by_head(x):
    low = lane_is_low(x.shape)
    zero = jnp.zeros_like(x)
    return jnp.where(low, x, zero), jnp.where(low, zero, x)


def pack_state(product):
    low = lane_is_low((HEAD_DIM, LANES))
    return jnp.where(low, product[:HEAD_DIM], product[HEAD_DIM:])


def unpack_state(state):
    low = lane_is_low(state.shape)
    zero = jnp.zeros_like(state)
    return jnp.concatenate([jnp.where(low, state, zero), jnp.where(low, zero, state)], axis=0)


def states_kernel(q_hbm, k_hbm, v_hbm, g_hbm, kv_ref, qg_ref, left_ref, right_ref, sems):
    copies = start_loads(q_hbm, k_hbm, v_hbm, g_hbm, left_ref, right_ref, sems)
    for out_ref, pair in ((kv_ref, 0), (qg_ref, 1)):
        wait_loads(copies, pair)
        for t in range(out_ref.shape[0] // HEAD_DIM):
            lanes = slice(t * LANES, (t + 1) * LANES)
            rows = slice(t * HEAD_DIM, (t + 1) * HEAD_DIM)
            out_ref[rows] = pack_state(dot(left_ref[pair, :, lanes], right_ref[pair, :, lanes], TN))


def start_loads(q_hbm, k_hbm, v_hbm, g_hbm, left_ref, right_ref, sems):
    copies = []
    for pair, (left, right) in enumerate(((k_hbm, v_hbm), (g_hbm, q_hbm))):
        copies.append(
            (
                pltpu.make_async_copy(left, left_ref.at[pair], sems.at[pair, 0]),
                pltpu.make_async_copy(right, right_ref.at[pair], sems.at[pair, 1]),
            )
        )
    for copy in (*copies[0], *copies[1]):
        copy.start()
    return copies


def wait_loads(copies, pair):
    for copy in copies[pair]:
        copy.wait()


def place_on(axis):
    index = lax.axis_index(axis)
    return index // (lax.axis_size(axis) // 2), index % 2


def halves_kernel(axis, *refs):
    q_hbm, k_hbm, v_hbm, g_hbm, a_mine, a_other, b_mine, b_other, left_ref, right_ref, sems = refs
    copies = start_loads(q_hbm, k_hbm, v_hbm, g_hbm, left_ref, right_ref, sems)
    upper, odd = place_on(axis)
    count = left_ref.shape[2] // LANES // 2
    wait_loads(copies, 0)
    wait_loads(copies, 1)
    outs = ((a_mine, upper, odd), (a_other, upper, 1 - odd), (b_mine, 1 - upper, odd), (b_other, 1 - upper, 1 - odd))
    for out_ref, pair, half in outs:
        for t in range(count):
            lanes = pl.ds(pl.multiple_of((half * count + t) * LANES, LANES), LANES)
            rows = slice(t * HEAD_DIM, (t + 1) * HEAD_DIM)
            out_ref[rows] = pack_state(dot(left_ref[pair, :, lanes], right_ref[pair, :, lanes], TN))


def whole_state(pieces, axis, is_qg):
    if len(pieces) == 1:
        return lambda t: pieces[0][t * HEAD_DIM : (t + 1) * HEAD_DIM]
    a_sum, a1, b_sum, b1, t_mine, t_other, got = pieces
    upper, odd = place_on(axis)
    is_a = upper == is_qg
    count = a_sum.shape[0] // HEAD_DIM

    def rows_of(t):
        rows = slice(t % count * HEAD_DIM, (t % count + 1) * HEAD_DIM)
        a_own = a_sum[rows] + jnp.where(odd != upper, a1[rows], 0.0)
        b_own = b_sum[rows] + jnp.where(odd == upper, b1[rows], 0.0) + t_mine[rows]
        other = got[rows] + jnp.where(is_a, 0.0, t_other[rows])
        return jnp.where(odd == t // count, jnp.where(is_a, a_own, b_own), other)

    return rows_of


def block_kernel(
    factor, q_ref, k_ref, v_ref, g_ref, gain_ref, out_ref, dq_ref, dk_ref, dv_ref, row_ref
):
    row_ref[...] = gain_ref[...]
    row = lax.broadcasted_iota(jnp.int32, (BLOCK, BLOCK), 0)
    column = lax.broadcasted_iota(jnp.int32, (BLOCK, BLOCK), 1)
    causal = row >= column
    for t in range(tiles(q_ref)):
        q, k, v, g = (tile(ref, t) for ref in (q_ref, k_ref, v_ref, g_ref))
        cols = slice(t * LANES, (t + 1) * LANES)
        out = dq = dk = dv = None
        for qh, gh, kh, vh in zip(by_head(q), by_head(g), by_head(k), by_head(v)):
            weights = (factor * jnp.where(causal, dot(qh, k, NT), 0.0)).astype(bf16)
            dweights = (factor * jnp.where(causal, dot(gh, v, NT), 0.0)).astype(bf16)
            parts = (dot(weights, vh), dot(dweights, kh), dot(dweights, qh, TN), dot(weights, gh, TN))
            if out is None:
                out, dq, dk, dv = parts
            else:
                out, dq, dk, dv = (x + y for x, y in zip((out, dq, dk, dv), parts))
        out_ref[:, cols] = out
        dq_ref[:, cols] = dq
        dk_ref[:, cols] = dk
        dv_ref[:, cols] = dv


def output_kernel(factor, axis, q_ref, part_ref, *refs):
    *pieces, out_ref, squares_ref = refs
    kv_of = whole_state(pieces, axis, 0)
    total = None
    for t in range(tiles(q_ref)):
        cols = slice(t * LANES, (t + 1) * LANES)
        state = unpack_state((factor * kv_of(t)).astype(bf16))
        out = part_ref[:, cols] + dot(tile(q_ref, t), state)
        out_ref[:, cols] = out
        square = out * out
        total = square if total is None else total + square
    squares_ref[...] = jnp.sum(total.T, axis=0, keepdims=True)


def grads_kernel(factor, axis, k_ref, v_ref, g_ref, dq_part, dk_part, dv_part, *refs):
    *pieces, dq_ref, dk_ref, dv_ref = refs
    kv_of = whole_state(pieces[: len(pieces) // 2], axis, 0)
    qg_of = whole_state(pieces[len(pieces) // 2 :], axis, 1)
    for t in range(tiles(k_ref)):
        cols = slice(t * LANES, (t + 1) * LANES)
        state = unpack_state((factor * kv_of(t)).astype(bf16))
        grad_state = unpack_state((factor * qg_of(t)).astype(bf16))
        dq_ref[:, cols] = (dq_part[:, cols] + dot(tile(g_ref, t), state, NT)).astype(bf16)
        dk_ref[:, cols] = (dk_part[:, cols] + dot(tile(v_ref, t), grad_state)).astype(bf16)
        dv_ref[:, cols] = (dv_part[:, cols] + dot(tile(k_ref, t), grad_state, NT)).astype(bf16)


def norm_kernel(width, out_ref, gain_ref, *refs):
    *shares, normed_ref = refs
    total = shares[0][...]
    for share in shares[1:]:
        total = total + share[...]
    scale = lax.rsqrt(total / width + epsilon)
    scale = jnp.broadcast_to(scale, (LANES, scale.shape[1])).T
    for t in range(tiles(out_ref)):
        cols = slice(t * LANES, (t + 1) * LANES)
        normed_ref[:, cols] = (out_ref[:, cols] * scale * gain_ref[:, cols]).astype(bf16)


def call(kernel, outs, args, flops, vmem=16 * MIB, **spec):
    moved = sum(math.prod(a.shape) * jnp.dtype(a.dtype).itemsize for a in (*args, *outs))
    whole = pl.BlockSpec(memory_space=pltpu.VMEM)
    single = len(outs) == 1
    return pl.pallas_call(
        kernel,
        out_shape=outs[0] if single else tuple(outs),
        in_specs=[pl.BlockSpec(memory_space=spec.pop("inputs_at", pltpu.VMEM))] * len(args),
        out_specs=whole if single else tuple([whole] * len(outs)),
        compiler_params=pltpu.CompilerParams(vmem_limit_bytes=vmem),
        cost_estimate=pl.CostEstimate(flops=flops, bytes_accessed=moved, transcendentals=0),
        **spec,
    )(*args)


def swap(x, axis, distance):
    size = lax.axis_size(axis)
    return lax.ppermute(x, axis, [(i, i ^ distance) for i in range(size)])


def scan_states(axis, states, halves):
    count = lax.axis_size(axis)
    index = lax.axis_index(axis)
    bit = lambda d: (index & d) != 0
    top = count // 2
    if count & (count - 1):
        kv, qg = states()
        position = jnp.arange(count)[:, None, None]
        every_kv = lax.all_gather(kv, axis)
        every_qg = lax.all_gather(qg, axis)
        before = jnp.sum(jnp.where(position < index, every_kv, 0.0), axis=0)
        after = jnp.sum(jnp.where(position > index, every_qg, 0.0), axis=0)
        return (before,), (after,)
    if count < 8:
        total_kv, total_qg = states()
        before, after = jnp.zeros_like(total_kv), jnp.zeros_like(total_qg)
        distance = 1
        while distance < count:
            got_kv, got_qg = swap(total_kv, axis, distance), swap(total_qg, axis, distance)
            before = before + jnp.where(bit(distance), got_kv, 0.0)
            after = after + jnp.where(bit(distance), 0.0, got_qg)
            total_kv, total_qg = total_kv + got_kv, total_qg + got_qg
            distance *= 2
        return (before,), (after,)
    upper = bit(top)
    a_enters = lambda d: bit(d) != upper
    b_enters = lambda d: bit(d) == upper

    def send(x, distance):
        return swap(x, axis, distance)

    a_mine, a_other, b_mine, b_other = halves()
    a3 = send(a_other, 3)
    a2 = send(a_mine, 2)
    a1 = send(a_other, 1)
    b3 = send(b_other, 3)
    b2 = send(b_mine, 2)
    b1 = send(b_other, 1)
    a_pair, b_pair = a2 + a3, b2 + b3
    a_in, b_in = lax.optimization_barrier((a_pair, b_pair))
    a_sum = jnp.where(a_enters(2), a_in, 0.0)
    b_sum = jnp.where(b_enters(2), b_in, 0.0)
    a_total = a_mine + a1 + a_pair
    b_total = b_mine + b1 + b_pair
    distance = 4
    while distance < top:
        a_got, b_got = send(a_total, distance), send(b_total, distance)
        a_sum = a_sum + jnp.where(a_enters(distance), a_got, 0.0)
        b_sum = b_sum + jnp.where(b_enters(distance), b_got, 0.0)
        a_total, b_total = a_total + a_got, b_total + b_got
        distance *= 2
    t_other = send(a_total, top | 1)
    t_mine = send(a_total, top)
    a_out = a_sum + jnp.where(a_enters(1), 0.0, a_mine)
    b_out = b_sum + jnp.where(b_enters(1), 0.0, b_mine)
    got_kv = send(jnp.where(upper, b_out, a_out), 1)
    got_qg = send(jnp.where(upper, a_out, b_out), 1)
    own = (a_sum, a1, b_sum, b1)
    return (*own, t_mine, t_other, got_kv), (*own, t_mine, t_other, got_qg)


def all_shares(row, axis):
    count = lax.axis_size(axis)
    if count & (count - 1):
        return [lax.psum(row, axis)]
    if count > 4:
        distance = 1
        while distance < count:
            row = row + swap(row, axis, distance)
            distance *= 2
        return [row]
    rows = [row]
    for distance in range(count - 1, 0, -1):
        rows.append(swap(row, axis, distance))
    return rows


def body(queries, keys, values, d_out, gain):
    length, width = queries.shape
    factor = 1.0 / math.sqrt(HEAD_DIM * length * lax.axis_size("seq"))
    packed = jax.ShapeDtypeStruct((width // LANES * HEAD_DIM, LANES), f32)
    wide = jax.ShapeDtypeStruct((length, width), f32)
    narrow = jax.ShapeDtypeStruct((length, width), bf16)
    inputs = (queries, keys, values, d_out)
    half = jax.ShapeDtypeStruct((packed.shape[0] // 2, LANES), f32)

    def products(kernel, outs):
        return call(
            kernel,
            outs,
            inputs,
            4 * length * LANES * width,
            vmem=64 * MIB - 10600 * 1024,
            inputs_at=pltpu.HBM,
            scratch_shapes=[pltpu.VMEM((2, length, width), bf16)] * 2
            + [pltpu.SemaphoreType.DMA((2, 2))],
        )

    out_part, dq_part, dk_part, dv_part, gain_row = call(
        functools.partial(block_kernel, factor),
        [wide] * 4 + [jax.ShapeDtypeStruct((1, width), f32)],
        (*inputs, gain[None]),
        24 * length * LANES * width,
    )
    kv_pieces, qg_pieces = scan_states(
        "seq",
        lambda: products(states_kernel, [packed] * 2),
        lambda: products(functools.partial(halves_kernel, "seq"), [half] * 4),
    )
    out, squares = call(
        functools.partial(output_kernel, factor, "seq"),
        [wide, jax.ShapeDtypeStruct((1, length), f32)],
        (queries, out_part, *kv_pieces),
        2 * length * LANES * width,
    )
    shares = all_shares(squares, "head")
    dq, dk, dv = call(
        functools.partial(grads_kernel, factor, "seq"),
        [narrow] * 3,
        (keys, values, d_out, dq_part, dk_part, dv_part, *kv_pieces, *qg_pieces),
        6 * length * LANES * width,
    )
    normed = call(
        functools.partial(norm_kernel, width * lax.axis_size("head")),
        [narrow],
        (out, gain_row, *shares),
        2 * length * width,
    )
    return normed, dq, dk, dv


def solution(mesh):
    placed = (P("seq", "head"), P("seq", "head"), P("seq", "head"), P("seq", "head"), P("head"))

    return jax.shard_map(
        body,
        mesh=mesh,
        in_specs=placed,
        out_specs=(P("seq", "head"), P("seq", "head"), P("seq", "head"), P("seq", "head")),
        check_vma=False,
    )
```

```python
import functools
import math

import jax
import jax.numpy as jnp
from jax import lax
from jax.experimental import pallas as pl
from jax.experimental.pallas import tpu as pltpu
from jax.sharding import PartitionSpec as P


HEAD_DIM = 64
BLOCK = 128
LANES = 128
MIB = 2**20

epsilon = 1e-06


f32 = jnp.float32
bf16 = jnp.bfloat16


def dot(x, y, dims=((1,), (0,))):
    return lax.dot_general(x, y, (dims, ((), ())), preferred_element_type=f32)


NT = ((1,), (1,))
TN = ((0,), (0,))


def tiles(ref):
    return ref.shape[1] // LANES


def tile(ref, t):
    return ref[:, t * LANES : (t + 1) * LANES]


def lane_is_low(shape):
    return lax.broadcasted_iota(jnp.int32, shape, 1) < HEAD_DIM


def by_head(x):
    low = lane_is_low(x.shape)
    zero = jnp.zeros_like(x)
    return jnp.where(low, x, zero), jnp.where(low, zero, x)


def pack_state(product):
    low = lane_is_low((HEAD_DIM, LANES))
    return jnp.where(low, product[:HEAD_DIM], product[HEAD_DIM:])


def unpack_state(state):
    low = lane_is_low(state.shape)
    zero = jnp.zeros_like(state)
    return jnp.concatenate([jnp.where(low, state, zero), jnp.where(low, zero, state)], axis=0)


def states_kernel(q_hbm, k_hbm, v_hbm, g_hbm, kv_ref, qg_ref, left_ref, right_ref, sems):
    copies = start_loads(q_hbm, k_hbm, v_hbm, g_hbm, left_ref, right_ref, sems)
    for out_ref, pair in ((kv_ref, 0), (qg_ref, 1)):
        wait_loads(copies, pair)
        for t in range(out_ref.shape[0] // HEAD_DIM):
            lanes = slice(t * LANES, (t + 1) * LANES)
            rows = slice(t * HEAD_DIM, (t + 1) * HEAD_DIM)
            out_ref[rows] = pack_state(dot(left_ref[pair, :, lanes], right_ref[pair, :, lanes], TN))


def start_loads(q_hbm, k_hbm, v_hbm, g_hbm, left_ref, right_ref, sems):
    copies = []
    for pair, (left, right) in enumerate(((k_hbm, v_hbm), (g_hbm, q_hbm))):
        copies.append(
            (
                pltpu.make_async_copy(left, left_ref.at[pair], sems.at[pair, 0]),
                pltpu.make_async_copy(right, right_ref.at[pair], sems.at[pair, 1]),
            )
        )
    for copy in (*copies[0], *copies[1]):
        copy.start()
    return copies


def wait_loads(copies, pair):
    for copy in copies[pair]:
        copy.wait()


def place_on(axis):
    index = lax.axis_index(axis)
    return index // (lax.axis_size(axis) // 2), index % 2


def halves_kernel(axis, *refs):
    q_hbm, k_hbm, v_hbm, g_hbm, a_mine, a_other, b_mine, b_other, left_ref, right_ref, sems = refs
    copies = start_loads(q_hbm, k_hbm, v_hbm, g_hbm, left_ref, right_ref, sems)
    upper, odd = place_on(axis)
    count = left_ref.shape[2] // LANES // 2
    wait_loads(copies, 0)
    wait_loads(copies, 1)
    outs = ((a_mine, upper, odd), (a_other, upper, 1 - odd), (b_mine, 1 - upper, odd), (b_other, 1 - upper, 1 - odd))
    for out_ref, pair, half in outs:
        for t in range(count):
            lanes = pl.ds(pl.multiple_of((half * count + t) * LANES, LANES), LANES)
            rows = slice(t * HEAD_DIM, (t + 1) * HEAD_DIM)
            out_ref[rows] = pack_state(dot(left_ref[pair, :, lanes], right_ref[pair, :, lanes], TN))


def whole_state(pieces, axis, is_qg):
    if len(pieces) == 1:
        return lambda t: pieces[0][t * HEAD_DIM : (t + 1) * HEAD_DIM]
    a_sum, a1, b_sum, b1, t_mine, t_other, got = pieces
    upper, odd = place_on(axis)
    is_a = upper == is_qg
    swapped = lax.axis_index("head") % 2 == 1
    count = a_sum.shape[0] // HEAD_DIM

    def rows_of(t):
        rows = slice(t % count * HEAD_DIM, (t % count + 1) * HEAD_DIM)
        a_own = a_sum[rows] + jnp.where(odd != upper, a1[rows], 0.0)
        b_own = b_sum[rows] + jnp.where(odd == upper, b1[rows], 0.0)
        b_own = b_own + jnp.where(swapped, t_other[rows], t_mine[rows])
        t_rows = jnp.where(swapped, t_mine[rows], t_other[rows])
        other = got[rows] + jnp.where(is_a, 0.0, t_rows)
        return jnp.where(odd == t // count, jnp.where(is_a, a_own, b_own), other)

    return rows_of


def block_kernel(
    factor, q_ref, k_ref, v_ref, g_ref, gain_ref, out_ref, dq_ref, dk_ref, dv_ref, row_ref
):
    row_ref[...] = gain_ref[...]
    row = lax.broadcasted_iota(jnp.int32, (BLOCK, BLOCK), 0)
    column = lax.broadcasted_iota(jnp.int32, (BLOCK, BLOCK), 1)
    causal = row >= column
    for t in range(tiles(q_ref)):
        q, k, v, g = (tile(ref, t) for ref in (q_ref, k_ref, v_ref, g_ref))
        cols = slice(t * LANES, (t + 1) * LANES)
        out = dq = dk = dv = None
        for qh, gh, kh, vh in zip(by_head(q), by_head(g), by_head(k), by_head(v)):
            weights = (factor * jnp.where(causal, dot(qh, k, NT), 0.0)).astype(bf16)
            dweights = (factor * jnp.where(causal, dot(gh, v, NT), 0.0)).astype(bf16)
            parts = (dot(weights, vh), dot(dweights, kh), dot(dweights, qh, TN), dot(weights, gh, TN))
            if out is None:
                out, dq, dk, dv = parts
            else:
                out, dq, dk, dv = (x + y for x, y in zip((out, dq, dk, dv), parts))
        out_ref[:, cols] = out
        dq_ref[:, cols] = dq
        dk_ref[:, cols] = dk
        dv_ref[:, cols] = dv


def output_kernel(factor, axis, q_ref, part_ref, *refs):
    *pieces, out_ref, squares_ref = refs
    kv_of = whole_state(pieces, axis, 0)
    total = None
    for t in range(tiles(q_ref)):
        cols = slice(t * LANES, (t + 1) * LANES)
        state = unpack_state((factor * kv_of(t)).astype(bf16))
        out = part_ref[:, cols] + dot(tile(q_ref, t), state)
        out_ref[:, cols] = out
        square = out * out
        total = square if total is None else total + square
    squares_ref[...] = jnp.sum(total.T, axis=0, keepdims=True)


def grads_kernel(factor, axis, k_ref, v_ref, g_ref, dq_part, dk_part, dv_part, *refs):
    *pieces, dq_ref, dk_ref, dv_ref = refs
    kv_of = whole_state(pieces[: len(pieces) // 2], axis, 0)
    qg_of = whole_state(pieces[len(pieces) // 2 :], axis, 1)
    for t in range(tiles(k_ref)):
        cols = slice(t * LANES, (t + 1) * LANES)
        state = unpack_state((factor * kv_of(t)).astype(bf16))
        grad_state = unpack_state((factor * qg_of(t)).astype(bf16))
        dq_ref[:, cols] = (dq_part[:, cols] + dot(tile(g_ref, t), state, NT)).astype(bf16)
        dk_ref[:, cols] = (dk_part[:, cols] + dot(tile(v_ref, t), grad_state)).astype(bf16)
        dv_ref[:, cols] = (dv_part[:, cols] + dot(tile(k_ref, t), grad_state, NT)).astype(bf16)


def norm_kernel(width, out_ref, gain_ref, *refs):
    *shares, normed_ref = refs
    total = shares[0][...]
    for share in shares[1:]:
        total = total + share[...]
    scale = lax.rsqrt(total / width + epsilon)
    scale = jnp.broadcast_to(scale, (LANES, scale.shape[1])).T
    for t in range(tiles(out_ref)):
        cols = slice(t * LANES, (t + 1) * LANES)
        normed_ref[:, cols] = (out_ref[:, cols] * scale * gain_ref[:, cols]).astype(bf16)


def call(kernel, outs, args, flops, vmem=16 * MIB, **spec):
    moved = sum(math.prod(a.shape) * jnp.dtype(a.dtype).itemsize for a in (*args, *outs))
    whole = pl.BlockSpec(memory_space=pltpu.VMEM)
    single = len(outs) == 1
    return pl.pallas_call(
        kernel,
        out_shape=outs[0] if single else tuple(outs),
        in_specs=[pl.BlockSpec(memory_space=spec.pop("inputs_at", pltpu.VMEM))] * len(args),
        out_specs=whole if single else tuple([whole] * len(outs)),
        compiler_params=pltpu.CompilerParams(vmem_limit_bytes=vmem),
        cost_estimate=pl.CostEstimate(flops=flops, bytes_accessed=moved, transcendentals=0),
        **spec,
    )(*args)


def swap(x, axis, distance):
    size = lax.axis_size(axis)
    return lax.ppermute(x, axis, [(i, i ^ distance) for i in range(size)])


def scan_states(axis, states, halves):
    count = lax.axis_size(axis)
    index = lax.axis_index(axis)
    bit = lambda d: (index & d) != 0
    top = count // 2
    if count & (count - 1):
        kv, qg = states()
        position = jnp.arange(count)[:, None, None]
        every_kv = lax.all_gather(kv, axis)
        every_qg = lax.all_gather(qg, axis)
        before = jnp.sum(jnp.where(position < index, every_kv, 0.0), axis=0)
        after = jnp.sum(jnp.where(position > index, every_qg, 0.0), axis=0)
        return (before,), (after,)
    if count < 8:
        total_kv, total_qg = states()
        before, after = jnp.zeros_like(total_kv), jnp.zeros_like(total_qg)
        distance = 1
        while distance < count:
            got_kv, got_qg = swap(total_kv, axis, distance), swap(total_qg, axis, distance)
            before = before + jnp.where(bit(distance), got_kv, 0.0)
            after = after + jnp.where(bit(distance), 0.0, got_qg)
            total_kv, total_qg = total_kv + got_kv, total_qg + got_qg
            distance *= 2
        return (before,), (after,)
    upper = bit(top)
    a_enters = lambda d: bit(d) != upper
    b_enters = lambda d: bit(d) == upper

    def send(x, distance):
        return swap(x, axis, distance)

    def send_by_core(x, distances):
        heads = lax.axis_size("head")
        pairs = [
            (i * heads + h, (i ^ distances[h % 2]) * heads + h) for i in range(count) for h in range(heads)
        ]
        return lax.ppermute(x, (axis, "head"), pairs)

    a_mine, a_other, b_mine, b_other = halves()
    a3 = send(a_other, 3)
    a2 = send(a_mine, 2)
    a1 = send(a_other, 1)
    b3 = send(b_other, 3)
    b2 = send(b_mine, 2)
    b1 = send(b_other, 1)
    a_pair, b_pair = a2 + a3, b2 + b3
    a_in, b_in = lax.optimization_barrier((a_pair, b_pair))
    a_sum = jnp.where(a_enters(2), a_in, 0.0)
    b_sum = jnp.where(b_enters(2), b_in, 0.0)
    a_total = a_mine + a1 + a_pair
    b_total = b_mine + b1 + b_pair
    distance = 4
    while distance < top:
        a_got, b_got = send(a_total, distance), send(b_total, distance)
        a_sum = a_sum + jnp.where(a_enters(distance), a_got, 0.0)
        b_sum = b_sum + jnp.where(b_enters(distance), b_got, 0.0)
        a_total, b_total = a_total + a_got, b_total + b_got
        distance *= 2
    t_other = send_by_core(a_total, (top | 1, top))
    t_mine = send_by_core(a_total, (top, top | 1))
    a_out = a_sum + jnp.where(a_enters(1), 0.0, a_mine)
    b_out = b_sum + jnp.where(b_enters(1), 0.0, b_mine)
    got_kv = send(jnp.where(upper, b_out, a_out), 1)
    got_qg = send(jnp.where(upper, a_out, b_out), 1)
    own = (a_sum, a1, b_sum, b1)
    return (*own, t_mine, t_other, got_kv), (*own, t_mine, t_other, got_qg)


def all_shares(row, axis):
    count = lax.axis_size(axis)
    if count & (count - 1):
        return [lax.psum(row, axis)]
    if count > 4:
        distance = 1
        while distance < count:
            row = row + swap(row, axis, distance)
            distance *= 2
        return [row]
    rows = [row]
    for distance in range(count - 1, 0, -1):
        rows.append(swap(row, axis, distance))
    return rows


def body(queries, keys, values, d_out, gain):
    length, width = queries.shape
    factor = 1.0 / math.sqrt(HEAD_DIM * length * lax.axis_size("seq"))
    packed = jax.ShapeDtypeStruct((width // LANES * HEAD_DIM, LANES), f32)
    wide = jax.ShapeDtypeStruct((length, width), f32)
    narrow = jax.ShapeDtypeStruct((length, width), bf16)
    inputs = (queries, keys, values, d_out)
    half = jax.ShapeDtypeStruct((packed.shape[0] // 2, LANES), f32)

    def products(kernel, outs):
        return call(
            kernel,
            outs,
            inputs,
            4 * length * LANES * width,
            vmem=64 * MIB - 10600 * 1024,
            inputs_at=pltpu.HBM,
            scratch_shapes=[pltpu.VMEM((2, length, width), bf16)] * 2
            + [pltpu.SemaphoreType.DMA((2, 2))],
        )

    out_part, dq_part, dk_part, dv_part, gain_row = call(
        functools.partial(block_kernel, factor),
        [wide] * 4 + [jax.ShapeDtypeStruct((1, width), f32)],
        (*inputs, gain[None]),
        24 * length * LANES * width,
    )
    kv_pieces, qg_pieces = scan_states(
        "seq",
        lambda: products(states_kernel, [packed] * 2),
        lambda: products(functools.partial(halves_kernel, "seq"), [half] * 4),
    )
    out, squares = call(
        functools.partial(output_kernel, factor, "seq"),
        [wide, jax.ShapeDtypeStruct((1, length), f32)],
        (queries, out_part, *kv_pieces),
        2 * length * LANES * width,
    )
    shares = all_shares(squares, "head")
    dq, dk, dv = call(
        functools.partial(grads_kernel, factor, "seq"),
        [narrow] * 3,
        (keys, values, d_out, dq_part, dk_part, dv_part, *kv_pieces, *qg_pieces),
        6 * length * LANES * width,
    )
    normed = call(
        functools.partial(norm_kernel, width * lax.axis_size("head")),
        [narrow],
        (out, gain_row, *shares),
        2 * length * width,
    )
    return normed, dq, dk, dv


def solution(mesh):
    placed = (P("seq", "head"), P("seq", "head"), P("seq", "head"), P("seq", "head"), P("head"))

    return jax.shard_map(
        body,
        mesh=mesh,
        in_specs=placed,
        out_specs=(P("seq", "head"), P("seq", "head"), P("seq", "head"), P("seq", "head")),
        check_vma=False,
    )
```

```python
import functools
import math

import jax
import jax.numpy as jnp
from jax import lax
from jax.experimental import pallas as pl
from jax.experimental.pallas import tpu as pltpu
from jax.sharding import PartitionSpec as P


HEAD_DIM = 64
BLOCK = 128
LANES = 128
MIB = 2**20

epsilon = 1e-06


f32 = jnp.float32
bf16 = jnp.bfloat16


def dot(x, y, dims=((1,), (0,))):
    return lax.dot_general(x, y, (dims, ((), ())), preferred_element_type=f32)


NT = ((1,), (1,))
TN = ((0,), (0,))


def tiles(ref):
    return ref.shape[1] // LANES


def tile(ref, t):
    return ref[:, t * LANES : (t + 1) * LANES]


def lane_is_low(shape):
    return lax.broadcasted_iota(jnp.int32, shape, 1) < HEAD_DIM


def by_head(x):
    low = lane_is_low(x.shape)
    zero = jnp.zeros_like(x)
    return jnp.where(low, x, zero), jnp.where(low, zero, x)


def pack_state(product):
    low = lane_is_low((HEAD_DIM, LANES))
    return jnp.where(low, product[:HEAD_DIM], product[HEAD_DIM:])


def unpack_state(state):
    low = lane_is_low(state.shape)
    zero = jnp.zeros_like(state)
    return jnp.concatenate([jnp.where(low, state, zero), jnp.where(low, zero, state)], axis=0)


def states_kernel(q_hbm, k_hbm, v_hbm, g_hbm, kv_ref, qg_ref, left_ref, right_ref, sems):
    copies = start_loads(q_hbm, k_hbm, v_hbm, g_hbm, left_ref, right_ref, sems)
    for out_ref, pair in ((kv_ref, 0), (qg_ref, 1)):
        wait_loads(copies, pair)
        for t in range(out_ref.shape[0] // HEAD_DIM):
            lanes = slice(t * LANES, (t + 1) * LANES)
            rows = slice(t * HEAD_DIM, (t + 1) * HEAD_DIM)
            out_ref[rows] = pack_state(dot(left_ref[pair, :, lanes], right_ref[pair, :, lanes], TN))


def start_loads(q_hbm, k_hbm, v_hbm, g_hbm, left_ref, right_ref, sems):
    copies = []
    for pair, (left, right) in enumerate(((v_hbm, k_hbm), (g_hbm, q_hbm))):
        copies.append(
            (
                pltpu.make_async_copy(left, left_ref.at[pair], sems.at[pair, 0]),
                pltpu.make_async_copy(right, right_ref.at[pair], sems.at[pair, 1]),
            )
        )
    for copy in (*copies[0], *copies[1]):
        copy.start()
    return copies


def wait_loads(copies, pair):
    for copy in copies[pair]:
        copy.wait()


def place_on(axis):
    index = lax.axis_index(axis)
    return index // (lax.axis_size(axis) // 2), index % 2


def halves_kernel(axis, *refs):
    q_hbm, k_hbm, v_hbm, g_hbm, a_mine, a_other, b_mine, b_other, left_ref, right_ref, sems = refs
    copies = start_loads(q_hbm, k_hbm, v_hbm, g_hbm, left_ref, right_ref, sems)
    upper, odd = place_on(axis)
    count = left_ref.shape[2] // LANES // 2
    wait_loads(copies, 0)
    wait_loads(copies, 1)
    outs = ((a_mine, upper, odd), (a_other, upper, 1 - odd), (b_mine, 1 - upper, odd), (b_other, 1 - upper, 1 - odd))
    for out_ref, pair, half in outs:
        for t in range(count):
            lanes = pl.ds(pl.multiple_of((half * count + t) * LANES, LANES), LANES)
            rows = slice(t * HEAD_DIM, (t + 1) * HEAD_DIM)
            out_ref[rows] = pack_state(dot(left_ref[pair, :, lanes], right_ref[pair, :, lanes], TN))


def whole_state(pieces, axis, is_qg):
    if len(pieces) == 1:
        return lambda t: pieces[0][t * HEAD_DIM : (t + 1) * HEAD_DIM]
    a_sum, a1, b_sum, b1, t_mine, t_other, got = pieces
    upper, odd = place_on(axis)
    is_a = upper == is_qg
    count = a_sum.shape[0] // HEAD_DIM

    def rows_of(t):
        rows = slice(t % count * HEAD_DIM, (t % count + 1) * HEAD_DIM)
        a_own = a_sum[rows] + jnp.where(odd != upper, a1[rows], 0.0)
        b_own = b_sum[rows] + jnp.where(odd == upper, b1[rows], 0.0) + t_mine[rows]
        other = got[rows] + jnp.where(is_a, 0.0, t_other[rows])
        return jnp.where(odd == t // count, jnp.where(is_a, a_own, b_own), other)

    return rows_of


def block_kernel(
    factor, q_ref, k_ref, v_ref, g_ref, gain_ref, out_ref, dq_ref, dk_ref, dv_ref, row_ref
):
    row_ref[...] = gain_ref[...]
    row = lax.broadcasted_iota(jnp.int32, (BLOCK, BLOCK), 0)
    column = lax.broadcasted_iota(jnp.int32, (BLOCK, BLOCK), 1)
    causal = row >= column
    for t in range(tiles(q_ref)):
        q, k, v, g = (tile(ref, t) for ref in (q_ref, k_ref, v_ref, g_ref))
        cols = slice(t * LANES, (t + 1) * LANES)
        out = dq = dk = dv = None
        for qh, gh, kh, vh in zip(by_head(q), by_head(g), by_head(k), by_head(v)):
            weights = (factor * jnp.where(causal, dot(qh, k, NT), 0.0)).astype(bf16)
            dweights = (factor * jnp.where(causal, dot(gh, v, NT), 0.0)).astype(bf16)
            parts = (dot(vh, weights, ((0,), (1,))), dot(dweights, kh), dot(dweights, qh, TN), dot(weights, gh, TN))
            if out is None:
                out, dq, dk, dv = parts
            else:
                out, dq, dk, dv = (x + y for x, y in zip((out, dq, dk, dv), parts))
        out_ref[cols] = out
        dq_ref[:, cols] = dq
        dk_ref[:, cols] = dk
        dv_ref[:, cols] = dv


def output_kernel(factor, axis, q_ref, part_ref, *refs):
    *pieces, out_ref, squares_ref = refs
    kv_of = whole_state(pieces, axis, 0)
    total = None
    for t in range(tiles(q_ref)):
        cols = slice(t * LANES, (t + 1) * LANES)
        state = unpack_state((factor * kv_of(t)).astype(bf16))
        out = part_ref[cols] + dot(state, tile(q_ref, t), NT)
        out_ref[cols] = out
        square = out * out
        total = square if total is None else total + square
    squares_ref[...] = jnp.sum(total, axis=0, keepdims=True)


def grads_kernel(factor, axis, k_ref, v_ref, g_ref, dq_part, dk_part, dv_part, turned_ref, *refs):
    *pieces, dq_ref, dk_ref, dv_ref, out_ref = refs
    kv_of = whole_state(pieces[: len(pieces) // 2], axis, 0)
    qg_of = whole_state(pieces[len(pieces) // 2 :], axis, 1)
    for t in range(tiles(k_ref)):
        cols = slice(t * LANES, (t + 1) * LANES)
        state = unpack_state((factor * kv_of(t)).astype(bf16))
        grad_state = unpack_state((factor * qg_of(t)).astype(bf16))
        dq_ref[:, cols] = (dq_part[:, cols] + dot(tile(g_ref, t), state)).astype(bf16)
        dk_ref[:, cols] = (dk_part[:, cols] + dot(tile(v_ref, t), grad_state)).astype(bf16)
        dv_ref[:, cols] = (dv_part[:, cols] + dot(tile(k_ref, t), grad_state, NT)).astype(bf16)
        out_ref[:, cols] = turned_ref[cols].T


def norm_kernel(width, out_ref, gain_ref, *refs):
    *shares, normed_ref = refs
    total = shares[0][...]
    for share in shares[1:]:
        total = total + share[...]
    scale = lax.rsqrt(total / width + epsilon)
    scale = jnp.broadcast_to(scale, (LANES, scale.shape[1])).T
    for t in range(tiles(out_ref)):
        cols = slice(t * LANES, (t + 1) * LANES)
        normed_ref[:, cols] = (out_ref[:, cols] * scale * gain_ref[:, cols]).astype(bf16)


def call(kernel, outs, args, flops, vmem=16 * MIB, **spec):
    moved = sum(math.prod(a.shape) * jnp.dtype(a.dtype).itemsize for a in (*args, *outs))
    whole = pl.BlockSpec(memory_space=pltpu.VMEM)
    single = len(outs) == 1
    return pl.pallas_call(
        kernel,
        out_shape=outs[0] if single else tuple(outs),
        in_specs=[pl.BlockSpec(memory_space=spec.pop("inputs_at", pltpu.VMEM))] * len(args),
        out_specs=whole if single else tuple([whole] * len(outs)),
        compiler_params=pltpu.CompilerParams(vmem_limit_bytes=vmem),
        cost_estimate=pl.CostEstimate(flops=flops, bytes_accessed=moved, transcendentals=0),
        **spec,
    )(*args)


def swap(x, axis, distance):
    size = lax.axis_size(axis)
    return lax.ppermute(x, axis, [(i, i ^ distance) for i in range(size)])


def scan_states(axis, states, halves):
    count = lax.axis_size(axis)
    index = lax.axis_index(axis)
    bit = lambda d: (index & d) != 0
    top = count // 2
    if count & (count - 1):
        kv, qg = states()
        position = jnp.arange(count)[:, None, None]
        every_kv = lax.all_gather(kv, axis)
        every_qg = lax.all_gather(qg, axis)
        before = jnp.sum(jnp.where(position < index, every_kv, 0.0), axis=0)
        after = jnp.sum(jnp.where(position > index, every_qg, 0.0), axis=0)
        return (before,), (after,)
    if count < 8:
        total_kv, total_qg = states()
        before, after = jnp.zeros_like(total_kv), jnp.zeros_like(total_qg)
        distance = 1
        while distance < count:
            got_kv, got_qg = swap(total_kv, axis, distance), swap(total_qg, axis, distance)
            before = before + jnp.where(bit(distance), got_kv, 0.0)
            after = after + jnp.where(bit(distance), 0.0, got_qg)
            total_kv, total_qg = total_kv + got_kv, total_qg + got_qg
            distance *= 2
        return (before,), (after,)
    upper = bit(top)
    a_enters = lambda d: bit(d) != upper
    b_enters = lambda d: bit(d) == upper

    def send(x, distance):
        return swap(x, axis, distance)

    a_mine, a_other, b_mine, b_other = halves()
    a3 = send(a_other, 3)
    a2 = send(a_mine, 2)
    a1 = send(a_other, 1)
    b3 = send(b_other, 3)
    b2 = send(b_mine, 2)
    b1 = send(b_other, 1)
    a_pair, b_pair = a2 + a3, b2 + b3
    a_in, b_in = lax.optimization_barrier((a_pair, b_pair))
    a_sum = jnp.where(a_enters(2), a_in, 0.0)
    b_sum = jnp.where(b_enters(2), b_in, 0.0)
    a_total = a_mine + a1 + a_pair
    b_total = b_mine + b1 + b_pair
    distance = 4
    while distance < top:
        a_got, b_got = send(a_total, distance), send(b_total, distance)
        a_sum = a_sum + jnp.where(a_enters(distance), a_got, 0.0)
        b_sum = b_sum + jnp.where(b_enters(distance), b_got, 0.0)
        a_total, b_total = a_total + a_got, b_total + b_got
        distance *= 2
    t_other = send(a_total, top | 1)
    t_mine = send(a_total, top)
    a_out = a_sum + jnp.where(a_enters(1), 0.0, a_mine)
    b_out = b_sum + jnp.where(b_enters(1), 0.0, b_mine)
    got_kv = send(jnp.where(upper, b_out, a_out), 1)
    got_qg = send(jnp.where(upper, a_out, b_out), 1)
    own = (a_sum, a1, b_sum, b1)
    return (*own, t_mine, t_other, got_kv), (*own, t_mine, t_other, got_qg)


def all_shares(row, axis):
    count = lax.axis_size(axis)
    if count & (count - 1):
        return [lax.psum(row, axis)]
    if count > 4:
        distance = 1
        while distance < count:
            row = row + swap(row, axis, distance)
            distance *= 2
        return [row]
    rows = [row]
    for distance in range(count - 1, 0, -1):
        rows.append(swap(row, axis, distance))
    return rows


def body(queries, keys, values, d_out, gain):
    length, width = queries.shape
    factor = 1.0 / math.sqrt(HEAD_DIM * length * lax.axis_size("seq"))
    packed = jax.ShapeDtypeStruct((width // LANES * HEAD_DIM, LANES), f32)
    wide = jax.ShapeDtypeStruct((length, width), f32)
    narrow = jax.ShapeDtypeStruct((length, width), bf16)
    turned = jax.ShapeDtypeStruct((width, length), f32)
    inputs = (queries, keys, values, d_out)
    half = jax.ShapeDtypeStruct((packed.shape[0] // 2, LANES), f32)

    def products(kernel, outs):
        return call(
            kernel,
            outs,
            inputs,
            4 * length * LANES * width,
            vmem=64 * MIB - 10600 * 1024,
            inputs_at=pltpu.HBM,
            scratch_shapes=[pltpu.VMEM((2, length, width), bf16)] * 2
            + [pltpu.SemaphoreType.DMA((2, 2))],
        )

    out_part, dq_part, dk_part, dv_part, gain_row = call(
        functools.partial(block_kernel, factor),
        [turned] + [wide] * 3 + [jax.ShapeDtypeStruct((1, width), f32)],
        (*inputs, gain[None]),
        24 * length * LANES * width,
    )
    kv_pieces, qg_pieces = scan_states(
        "seq",
        lambda: products(states_kernel, [packed] * 2),
        lambda: products(functools.partial(halves_kernel, "seq"), [half] * 4),
    )
    turned_out, squares = call(
        functools.partial(output_kernel, factor, "seq"),
        [turned, jax.ShapeDtypeStruct((1, length), f32)],
        (queries, out_part, *kv_pieces),
        2 * length * LANES * width,
    )
    shares = all_shares(squares, "head")
    dq, dk, dv, out = call(
        functools.partial(grads_kernel, factor, "seq"),
        [narrow] * 3 + [wide],
        (keys, values, d_out, dq_part, dk_part, dv_part, turned_out, *kv_pieces, *qg_pieces),
        6 * length * LANES * width,
    )
    normed = call(
        functools.partial(norm_kernel, width * lax.axis_size("head")),
        [narrow],
        (out, gain_row, *shares),
        2 * length * width,
    )
    return normed, dq, dk, dv


def solution(mesh):
    placed = (P("seq", "head"), P("seq", "head"), P("seq", "head"), P("seq", "head"), P("head"))

    return jax.shard_map(
        body,
        mesh=mesh,
        in_specs=placed,
        out_specs=(P("seq", "head"), P("seq", "head"), P("seq", "head"), P("seq", "head")),
        check_vma=False,
    )
```

```python
import functools
import math

import jax
import jax.numpy as jnp
from jax import lax
from jax.experimental import pallas as pl
from jax.experimental.pallas import tpu as pltpu
from jax.sharding import PartitionSpec as P


HEAD_DIM = 64
BLOCK = 128
LANES = 128
MIB = 2**20

epsilon = 1e-06


f32 = jnp.float32
bf16 = jnp.bfloat16


def dot(x, y, dims=((1,), (0,))):
    return lax.dot_general(x, y, (dims, ((), ())), preferred_element_type=f32)


NT = ((1,), (1,))
TN = ((0,), (0,))


def tiles(ref):
    return ref.shape[1] // LANES


def tile(ref, t):
    return ref[:, t * LANES : (t + 1) * LANES]


def lane_is_low(shape):
    return lax.broadcasted_iota(jnp.int32, shape, 1) < HEAD_DIM


def by_head(x):
    low = lane_is_low(x.shape)
    zero = jnp.zeros_like(x)
    return jnp.where(low, x, zero), jnp.where(low, zero, x)


def pack_state(product):
    low = lane_is_low((HEAD_DIM, LANES))
    return jnp.where(low, product[:HEAD_DIM], product[HEAD_DIM:])


def unpack_state(state):
    low = lane_is_low(state.shape)
    zero = jnp.zeros_like(state)
    return jnp.concatenate([jnp.where(low, state, zero), jnp.where(low, zero, state)], axis=0)


def states_kernel(q_hbm, k_hbm, v_hbm, g_hbm, kv_ref, qg_ref, left_ref, right_ref, sems):
    copies = start_loads(q_hbm, k_hbm, v_hbm, g_hbm, left_ref, right_ref, sems)
    for out_ref, pair in ((kv_ref, 0), (qg_ref, 1)):
        wait_loads(copies, pair)
        for t in range(out_ref.shape[0] // HEAD_DIM):
            lanes = slice(t * LANES, (t + 1) * LANES)
            rows = slice(t * HEAD_DIM, (t + 1) * HEAD_DIM)
            out_ref[rows] = pack_state(dot(left_ref[pair, :, lanes], right_ref[pair, :, lanes], TN))


def start_loads(q_hbm, k_hbm, v_hbm, g_hbm, left_ref, right_ref, sems):
    copies = []
    for pair, (left, right) in enumerate(((v_hbm, k_hbm), (g_hbm, q_hbm))):
        copies.append(
            (
                pltpu.make_async_copy(left, left_ref.at[pair], sems.at[pair, 0]),
                pltpu.make_async_copy(right, right_ref.at[pair], sems.at[pair, 1]),
            )
        )
    for copy in (*copies[0], *copies[1]):
        copy.start()
    return copies


def wait_loads(copies, pair):
    for copy in copies[pair]:
        copy.wait()


def place_on(axis):
    index = lax.axis_index(axis)
    return index // (lax.axis_size(axis) // 2), index % 2


def halves_kernel(axis, *refs):
    q_hbm, k_hbm, v_hbm, g_hbm, a_mine, a_other, b_mine, b_other, left_ref, right_ref, sems = refs
    copies = start_loads(q_hbm, k_hbm, v_hbm, g_hbm, left_ref, right_ref, sems)
    upper, odd = place_on(axis)
    count = left_ref.shape[2] // LANES // 2
    wait_loads(copies, 0)
    wait_loads(copies, 1)
    outs = ((a_mine, upper, odd), (a_other, upper, 1 - odd), (b_mine, 1 - upper, odd), (b_other, 1 - upper, 1 - odd))
    for out_ref, pair, half in outs:
        for t in range(count):
            lanes = pl.ds(pl.multiple_of((half * count + t) * LANES, LANES), LANES)
            rows = slice(t * HEAD_DIM, (t + 1) * HEAD_DIM)
            out_ref[rows] = pack_state(dot(left_ref[pair, :, lanes], right_ref[pair, :, lanes], TN))


def whole_state(pieces, axis, is_qg):
    if len(pieces) == 1:
        return lambda t: pieces[0][t * HEAD_DIM : (t + 1) * HEAD_DIM]
    a_sum, a1, b_sum, b1, t_mine, t_other, got = pieces
    upper, odd = place_on(axis)
    is_a = upper == is_qg
    swapped = lax.axis_index("head") % 2 == 1
    count = a_sum.shape[0] // HEAD_DIM

    def rows_of(t):
        rows = slice(t % count * HEAD_DIM, (t % count + 1) * HEAD_DIM)
        a_own = a_sum[rows] + jnp.where(odd != upper, a1[rows], 0.0)
        b_own = b_sum[rows] + jnp.where(odd == upper, b1[rows], 0.0)
        b_own = b_own + jnp.where(swapped, t_other[rows], t_mine[rows])
        t_rows = jnp.where(swapped, t_mine[rows], t_other[rows])
        other = got[rows] + jnp.where(is_a, 0.0, t_rows)
        return jnp.where(odd == t // count, jnp.where(is_a, a_own, b_own), other)

    return rows_of


def block_kernel(
    factor, q_ref, k_ref, v_ref, g_ref, gain_ref, out_ref, dq_ref, dk_ref, dv_ref, row_ref
):
    row_ref[...] = gain_ref[...]
    row = lax.broadcasted_iota(jnp.int32, (BLOCK, BLOCK), 0)
    column = lax.broadcasted_iota(jnp.int32, (BLOCK, BLOCK), 1)
    causal = row >= column
    for t in range(tiles(q_ref)):
        q, k, v, g = (tile(ref, t) for ref in (q_ref, k_ref, v_ref, g_ref))
        cols = slice(t * LANES, (t + 1) * LANES)
        out = dq = dk = dv = None
        for qh, gh, kh, vh in zip(by_head(q), by_head(g), by_head(k), by_head(v)):
            weights = (factor * jnp.where(causal, dot(qh, k, NT), 0.0)).astype(bf16)
            dweights = (factor * jnp.where(causal, dot(gh, v, NT), 0.0)).astype(bf16)
            parts = (dot(vh, weights, ((0,), (1,))), dot(dweights, kh), dot(dweights, qh, TN), dot(weights, gh, TN))
            if out is None:
                out, dq, dk, dv = parts
            else:
                out, dq, dk, dv = (x + y for x, y in zip((out, dq, dk, dv), parts))
        out_ref[cols] = out
        dq_ref[:, cols] = dq
        dk_ref[:, cols] = dk
        dv_ref[:, cols] = dv


def output_kernel(factor, axis, q_ref, part_ref, *refs):
    *pieces, out_ref, squares_ref = refs
    kv_of = whole_state(pieces, axis, 0)
    total = None
    for t in range(tiles(q_ref)):
        cols = slice(t * LANES, (t + 1) * LANES)
        state = unpack_state((factor * kv_of(t)).astype(bf16))
        out = part_ref[cols] + dot(state, tile(q_ref, t), NT)
        out_ref[cols] = out
        square = out * out
        total = square if total is None else total + square
    squares_ref[...] = jnp.sum(total, axis=0, keepdims=True)


def grads_kernel(factor, axis, k_ref, v_ref, g_ref, dq_part, dk_part, dv_part, turned_ref, *refs):
    *pieces, dq_ref, dk_ref, dv_ref, out_ref = refs
    kv_of = whole_state(pieces[: len(pieces) // 2], axis, 0)
    qg_of = whole_state(pieces[len(pieces) // 2 :], axis, 1)
    for t in range(tiles(k_ref)):
        cols = slice(t * LANES, (t + 1) * LANES)
        state = unpack_state((factor * kv_of(t)).astype(bf16))
        grad_state = unpack_state((factor * qg_of(t)).astype(bf16))
        dq_ref[:, cols] = (dq_part[:, cols] + dot(tile(g_ref, t), state)).astype(bf16)
        dk_ref[:, cols] = (dk_part[:, cols] + dot(tile(v_ref, t), grad_state)).astype(bf16)
        dv_ref[:, cols] = (dv_part[:, cols] + dot(tile(k_ref, t), grad_state, NT)).astype(bf16)
        out_ref[:, cols] = turned_ref[cols].T


def norm_kernel(width, out_ref, gain_ref, *refs):
    *shares, normed_ref = refs
    total = shares[0][...]
    for share in shares[1:]:
        total = total + share[...]
    scale = lax.rsqrt(total / width + epsilon)
    scale = jnp.broadcast_to(scale, (LANES, scale.shape[1])).T
    for t in range(tiles(out_ref)):
        cols = slice(t * LANES, (t + 1) * LANES)
        normed_ref[:, cols] = (out_ref[:, cols] * scale * gain_ref[:, cols]).astype(bf16)


def call(kernel, outs, args, flops, vmem=16 * MIB, **spec):
    moved = sum(math.prod(a.shape) * jnp.dtype(a.dtype).itemsize for a in (*args, *outs))
    whole = pl.BlockSpec(memory_space=pltpu.VMEM)
    single = len(outs) == 1
    return pl.pallas_call(
        kernel,
        out_shape=outs[0] if single else tuple(outs),
        in_specs=[pl.BlockSpec(memory_space=spec.pop("inputs_at", pltpu.VMEM))] * len(args),
        out_specs=whole if single else tuple([whole] * len(outs)),
        compiler_params=pltpu.CompilerParams(vmem_limit_bytes=vmem),
        cost_estimate=pl.CostEstimate(flops=flops, bytes_accessed=moved, transcendentals=0),
        **spec,
    )(*args)


def swap(x, axis, distance):
    size = lax.axis_size(axis)
    return lax.ppermute(x, axis, [(i, i ^ distance) for i in range(size)])


def scan_states(axis, states, halves):
    count = lax.axis_size(axis)
    index = lax.axis_index(axis)
    bit = lambda d: (index & d) != 0
    top = count // 2
    if count & (count - 1):
        kv, qg = states()
        position = jnp.arange(count)[:, None, None]
        every_kv = lax.all_gather(kv, axis)
        every_qg = lax.all_gather(qg, axis)
        before = jnp.sum(jnp.where(position < index, every_kv, 0.0), axis=0)
        after = jnp.sum(jnp.where(position > index, every_qg, 0.0), axis=0)
        return (before,), (after,)
    if count < 8:
        total_kv, total_qg = states()
        before, after = jnp.zeros_like(total_kv), jnp.zeros_like(total_qg)
        distance = 1
        while distance < count:
            got_kv, got_qg = swap(total_kv, axis, distance), swap(total_qg, axis, distance)
            before = before + jnp.where(bit(distance), got_kv, 0.0)
            after = after + jnp.where(bit(distance), 0.0, got_qg)
            total_kv, total_qg = total_kv + got_kv, total_qg + got_qg
            distance *= 2
        return (before,), (after,)
    upper = bit(top)
    a_enters = lambda d: bit(d) != upper
    b_enters = lambda d: bit(d) == upper

    def send(x, distance):
        return swap(x, axis, distance)

    def send_by_core(x, distances):
        heads = lax.axis_size("head")
        pairs = [
            (i * heads + h, (i ^ distances[h % 2]) * heads + h) for i in range(count) for h in range(heads)
        ]
        return lax.ppermute(x, (axis, "head"), pairs)

    a_mine, a_other, b_mine, b_other = halves()
    a3 = send(a_other, 3)
    a2 = send(a_mine, 2)
    a1 = send(a_other, 1)
    b3 = send(b_other, 3)
    b2 = send(b_mine, 2)
    b1 = send(b_other, 1)
    a_pair, b_pair = a2 + a3, b2 + b3
    a_in, b_in = lax.optimization_barrier((a_pair, b_pair))
    a_sum = jnp.where(a_enters(2), a_in, 0.0)
    b_sum = jnp.where(b_enters(2), b_in, 0.0)
    a_total = a_mine + a1 + a_pair
    b_total = b_mine + b1 + b_pair
    distance = 4
    while distance < top:
        a_got, b_got = send(a_total, distance), send(b_total, distance)
        a_sum = a_sum + jnp.where(a_enters(distance), a_got, 0.0)
        b_sum = b_sum + jnp.where(b_enters(distance), b_got, 0.0)
        a_total, b_total = a_total + a_got, b_total + b_got
        distance *= 2
    t_other = send_by_core(a_total, (top | 1, top))
    t_mine = send_by_core(a_total, (top, top | 1))
    a_out = a_sum + jnp.where(a_enters(1), 0.0, a_mine)
    b_out = b_sum + jnp.where(b_enters(1), 0.0, b_mine)
    got_kv = send(jnp.where(upper, b_out, a_out), 1)
    got_qg = send(jnp.where(upper, a_out, b_out), 1)
    own = (a_sum, a1, b_sum, b1)
    return (*own, t_mine, t_other, got_kv), (*own, t_mine, t_other, got_qg)


def all_shares(row, axis):
    count = lax.axis_size(axis)
    if count & (count - 1):
        return [lax.psum(row, axis)]
    if count > 4:
        distance = 1
        while distance < count:
            row = row + swap(row, axis, distance)
            distance *= 2
        return [row]
    rows = [row]
    for distance in range(count - 1, 0, -1):
        rows.append(swap(row, axis, distance))
    return rows


def body(queries, keys, values, d_out, gain):
    length, width = queries.shape
    factor = 1.0 / math.sqrt(HEAD_DIM * length * lax.axis_size("seq"))
    packed = jax.ShapeDtypeStruct((width // LANES * HEAD_DIM, LANES), f32)
    wide = jax.ShapeDtypeStruct((length, width), f32)
    narrow = jax.ShapeDtypeStruct((length, width), bf16)
    turned = jax.ShapeDtypeStruct((width, length), f32)
    inputs = (queries, keys, values, d_out)
    half = jax.ShapeDtypeStruct((packed.shape[0] // 2, LANES), f32)

    def products(kernel, outs):
        return call(
            kernel,
            outs,
            inputs,
            4 * length * LANES * width,
            vmem=64 * MIB - 10600 * 1024,
            inputs_at=pltpu.HBM,
            scratch_shapes=[pltpu.VMEM((2, length, width), bf16)] * 2
            + [pltpu.SemaphoreType.DMA((2, 2))],
        )

    out_part, dq_part, dk_part, dv_part, gain_row = call(
        functools.partial(block_kernel, factor),
        [turned] + [wide] * 3 + [jax.ShapeDtypeStruct((1, width), f32)],
        (*inputs, gain[None]),
        24 * length * LANES * width,
    )
    kv_pieces, qg_pieces = scan_states(
        "seq",
        lambda: products(states_kernel, [packed] * 2),
        lambda: products(functools.partial(halves_kernel, "seq"), [half] * 4),
    )
    turned_out, squares = call(
        functools.partial(output_kernel, factor, "seq"),
        [turned, jax.ShapeDtypeStruct((1, length), f32)],
        (queries, out_part, *kv_pieces),
        2 * length * LANES * width,
    )
    shares = all_shares(squares, "head")
    dq, dk, dv, out = call(
        functools.partial(grads_kernel, factor, "seq"),
        [narrow] * 3 + [wide],
        (keys, values, d_out, dq_part, dk_part, dv_part, turned_out, *kv_pieces, *qg_pieces),
        6 * length * LANES * width,
    )
    normed = call(
        functools.partial(norm_kernel, width * lax.axis_size("head")),
        [narrow],
        (out, gain_row, *shares),
        2 * length * width,
    )
    return normed, dq, dk, dv


def solution(mesh):
    placed = (P("seq", "head"), P("seq", "head"), P("seq", "head"), P("seq", "head"), P("head"))

    return jax.shard_map(
        body,
        mesh=mesh,
        in_specs=placed,
        out_specs=(P("seq", "head"), P("seq", "head"), P("seq", "head"), P("seq", "head")),
        check_vma=False,
    )
```
